128 devices in a mesh: gx: 16 (over z, y), gy: 8 (over x, core).
Axes of the slice: x: 4, y: 4, z: 4, core: 2. Of those that a mesh axis runs over, the one named last changes fastest.
Arguments:
- points: bfloat16 [1048576, 64], P(('gx', 'gy')), may hold values from -6 to 6
- send_order: int32 [1048576], P(('gx', 'gy')), may hold values from 0 to 8191, as said below
- place_order: int32 [1048576], P(('gx', 'gy')), may hold values from 0 to 8191, as said below
- sample_rows: int32 [1048576], P(('gx', 'gy')), may hold values from 0 to 8191, as said below
- sketch: bfloat16 [1024, 256], replicated, may hold values from -0.1875 to 0.1875
Outputs:
- leaf_basis: bfloat16 [1048576, 256], P(('gx', 'gy'))
- path_transfer: float32 [32768, 256], P(('gx', 'gy'))
The draws below stay inside these ranges and needn't reach their ends.
Inputs may be any that keep to these rules, and one draw needn't show every extreme that they name: `send_order`: each block of 8192 entries is a permutation of 0 to 8191. `place_order`: each block of 8192 entries is a permutation of 0 to 8191. `sample_rows`: entry j of a device's block is a local row of block j mod 128 of the leaf-ordered points.
All inputs are finite; a program needn't handle non-finite values.
Results may differ from the reference program's by a relative error of at most 0.04.
Values may be sent and summed in bfloat16 or wider, within the bound.
No kernel may reach another device: no remote copies, remote signals or barrier semaphores. Data moves between devices by JAX's collectives and lax.ppermute only.
A program may use at most 128 MiB of HBM per device.

```python
import math
import jax
import jax.numpy as jnp
from jax import lax

DIM = 64
RANK = 256
LEAF = 1024
NSAMP = 1024
LEAVES_DEV = 8
NDEV = 128
PTS_DEV = 8192
SAMP_DEV = 8192
PEER_ROWS = 64
NPTS = 1048576
XLEVELS = 7


def draw_send_order(key, part):
    keys = jax.random.split(jax.random.fold_in(key, 11), NDEV)
    return jax.vmap(lambda item: jax.random.permutation(item, PTS_DEV))(keys).reshape(-1).astype(jnp.int32)


def draw_place_order(key, part):
    keys = jax.random.split(jax.random.fold_in(key, 23), NDEV)
    return jax.vmap(lambda item: jax.random.permutation(item, PTS_DEV))(keys).reshape(-1).astype(jnp.int32)


def draw_sample_rows(key, part):
    values = jax.random.randint(jax.random.fold_in(key, 37), (NDEV * SAMP_DEV,), 0, PTS_DEV)
    return values.at[0].set(0).at[1].set(PTS_DEV - 1).astype(jnp.int32)


def levels(stream_key, shape, pieces, smallest, top_value):
    def one(dim, shards_of):
        steps = jax.random.uniform(jax.random.fold_in(jax.random.fold_in(stream_key, 6), dim), (shards_of,), jnp.float32, smallest / len(pieces), top_value / len(pieces))
        return jnp.repeat(jnp.exp(steps), shape[dim] // shards_of).reshape((-1,) + (1,) * (len(shape) - dim - 1))

    gain = one(*pieces[0])
    for cut in pieces[1:]:
        gain = gain * one(*cut)
    return gain


def bell_draw(own_key, extent, spread, limit, cuts=(), held_as=jnp.bfloat16):
    entries = spread * jax.random.normal(own_key, extent, jnp.float32)
    if cuts:
        entries = entries * levels(own_key, extent, cuts, -0.22, 0.18)
    return jnp.clip(entries, -limit, limit).astype(held_as)


def setup_inputs(seed: int = 0) -> dict:
    key_of = jax.random.split(jax.random.key(seed), 6)
    return {
        "points": bell_draw(key_of[0], (NPTS, DIM), 1.0, 6.0, ((0, 128),)),
        "send_order": draw_send_order(jax.random.fold_in(key_of[5], 71), 0),
        "place_order": draw_place_order(jax.random.fold_in(key_of[5], 71), 0),
        "sample_rows": draw_sample_rows(jax.random.fold_in(key_of[5], 71), 0),
        "sketch": bell_draw(key_of[4], (NSAMP, RANK), NSAMP ** -0.5, 0.1875),
    }


def compress_leaf(leaf_points, leaf_samples, sketch):
    cross = jnp.dot(leaf_points.astype(jnp.float32), leaf_samples.T.astype(jnp.float32), preferred_element_type=jnp.float32)
    left_sq = lax.optimization_barrier(jnp.sum(jnp.square(leaf_points.astype(jnp.float32)), axis=1))
    right_sq = lax.optimization_barrier(jnp.sum(jnp.square(leaf_samples.astype(jnp.float32)), axis=1))
    distance = left_sq[:, None] + right_sq[None, :] - 2.0 * cross
    kernel = jnp.exp(distance * (-4.0 / leaf_points.shape[1])).astype(jnp.bfloat16)
    sketched = jnp.dot(kernel.astype(jnp.float32), sketch.astype(jnp.float32), preferred_element_type=jnp.float32)
    gram = jnp.dot(sketched.T.astype(jnp.float32), sketched.astype(jnp.float32), precision=lax.Precision.HIGHEST, preferred_element_type=jnp.float32)
    factor = jnp.linalg.cholesky(gram)
    solved = jax.scipy.linalg.solve_triangular(factor, sketched.T, lower=True)
    basis = (solved.T * math.sqrt(leaf_points.shape[0])).astype(jnp.bfloat16)
    return (basis, gram)

def block_transfer(child_gram, parent_gram):
    child_low = jnp.linalg.cholesky(child_gram)
    parent_low = jnp.linalg.cholesky(parent_gram)
    return jax.scipy.linalg.solve_triangular(parent_low, child_low, lower=True).T

def reference(points, send_order, place_order, sample_rows, sketch):
    blocks = points.reshape(NDEV, PTS_DEV, DIM)
    outgoing = jax.vmap(lambda rows, order: rows[order])(blocks, send_order.reshape(NDEV, PTS_DEV))
    received = outgoing.reshape(NDEV, NDEV, PEER_ROWS, DIM).transpose(1, 0, 2, 3).reshape(NDEV, PTS_DEV, DIM)
    arranged = jax.vmap(lambda rows, order: rows[order])(received, place_order.reshape(NDEV, PTS_DEV))
    owners = jnp.arange(SAMP_DEV, dtype=jnp.int32) % NDEV
    samples = arranged[owners[None, :], sample_rows.reshape(NDEV, SAMP_DEV)]
    leaf_points = arranged.reshape(NDEV * LEAVES_DEV, LEAF, DIM)
    leaf_samples = samples.reshape(NDEV * LEAVES_DEV, NSAMP, DIM)
    basis, grams = lax.map(lambda pair: compress_leaf(pair[0], pair[1], sketch), (leaf_points, leaf_samples))
    group = lax.optimization_barrier(jnp.sum(grams.reshape(NDEV, LEAVES_DEV, RANK, RANK), axis=1))
    level_grams = [group]
    for level in range(XLEVELS):
        group = lax.optimization_barrier(jnp.sum(group.reshape(-1, 2, RANK, RANK), axis=1))
        level_grams.append(jnp.repeat(group, 2 ** (level + 1), axis=0))
    path = jnp.zeros((NDEV, RANK, RANK), jnp.float32)
    for level in range(XLEVELS):
        path = path + jax.vmap(block_transfer)(level_grams[level], level_grams[level + 1])
    return (basis.reshape(NPTS, RANK), path.reshape(NDEV * RANK, RANK))
```

```python
import math

import jax
import jax.numpy as jnp
from jax import lax
from jax.experimental import pallas as pl
from jax.experimental.pallas import tpu as pltpu
from jax.sharding import PartitionSpec as P

LEAF = 1024
NSAMP = 1024
FEAT = 64
RANK = 256
HALF = 128
PANEL = 32
STEP = 8
BATCH = 8
CHUNK = 512
LOG2E = 1.4426950408889634
F32 = jnp.float32
BF16 = jnp.bfloat16


def split2(x):
    hi = x.astype(BF16)
    return hi, (x - hi.astype(F32)).astype(BF16)


def split3(x):
    hi = x.astype(BF16)
    rest = x - hi.astype(F32)
    mid = rest.astype(BF16)
    return hi, mid, (rest - mid.astype(F32)).astype(BF16)


def eliminate(rows):
    count = len(rows)
    rows = list(rows)
    shape = rows[0].shape

    def lane(row, at):
        return jnp.broadcast_to(row[:, at : at + 1], shape)

    for base in range(0, count, STEP):
        reach = min(2 * STEP, count - base)
        local = rows[base : base + STEP]
        coef = [
            [lane(local[i], base + j) if j >= i else None for j in range(reach)]
            for i in range(STEP)
        ]
        done = []
        for c in range(STEP):
            inv = lax.rsqrt(coef[c][c])
            for j in range(c + 1, reach):
                coef[c][j] = coef[c][j] * inv
            scaled = local[c] * inv
            done.append(scaled)
            for i in range(c + 1, STEP):
                for j in range(i, reach):
                    coef[i][j] = coef[i][j] - coef[c][i] * coef[c][j]
                local[i] = local[i] - coef[c][i] * scaled
        rows[base : base + STEP] = done
        for i in range(base + STEP, count):
            for c in range(STEP):
                factor = coef[c][i - base] if i - base < reach else lane(done[c], i)
                rows[i] = rows[i] - factor * done[c]
    return rows


def factor_all(work, diag, keep=None):
    lanes = lax.broadcasted_iota(jnp.int32, (BATCH, HALF), 1)
    for panel in range(RANK // PANEL):
        start = panel * PANEL
        half, offset = divmod(start, HALF)
        rows = []
        for i in range(PANEL):
            row = work[half, pl.ds(start + i, BATCH, stride=RANK), :]
            if offset:
                row = pltpu.roll(row, HALF - offset, 1)
            unit = jnp.where((lanes & (PANEL - 1)) == i, 1.0, 0.0)
            rows.append(jnp.where(lanes < PANEL, row, unit))
        rows = eliminate(rows)
        for i in range(PANEL):
            diag[pl.ds(i, BATCH, stride=PANEL), :] = rows[i]
        group = lax.broadcasted_iota(jnp.int32, (PANEL, HALF), 1) // PANEL
        in_panel = lax.broadcasted_iota(jnp.int32, (PANEL, HALF), 1) - offset
        at_row = lax.broadcasted_iota(jnp.int32, (PANEL, HALF), 0)
        for m in range(BATCH):
            block = diag[m * PANEL : (m + 1) * PANEL, :]
            if keep is not None:
                keep[panel, m * PANEL : (m + 1) * PANEL, :] = block
            hi, mid, low = split3(block)
            hi, mid, low = (v.astype(F32) for v in (hi, mid, low))
            zero = jnp.zeros_like(hi)
            first = jnp.where(group == 0, zero, hi).astype(BF16)
            second = jnp.where(
                group == 0, zero, jnp.where(group == 3, low, mid)
            ).astype(BF16)
            left = jnp.concatenate([first, second], axis=1)
            base = m * RANK
            fresh = []
            for h in range(2):
                top = work[h, base + start : base + start + PANEL, :]
                if h == half:
                    inside = (in_panel >= 0) & (in_panel < PANEL)
                    top = jnp.where(inside, jnp.where(in_panel == at_row, 1.0, 0.0), top)
                th, tm, tl = split3(top)
                tz = jnp.zeros_like(th)
                right = jnp.concatenate([tz, th, tm, tl, tz, th, tm, th], axis=0)
                new = jnp.dot(left, right, preferred_element_type=F32)
                work[h, base + start : base + start + PANEL, :] = new
                fresh.append(new)
            after = start + PANEL
            if after == RANK:
                continue
            parts = [split3(v) for v in fresh]
            for h in range(2):
                lo_row = max(after, h * HALF)
                hi_row = (h + 1) * HALF
                if lo_row >= hi_row:
                    continue
                ah, am, al = parts[h]
                lhs = jnp.concatenate([ah, ah, am, ah, am, al], axis=0)
                for g in range(2):
                    bh, bm, bl = parts[g]
                    rhs = jnp.concatenate([bh, bm, bh, bl, bm, bh], axis=0)
                    prod = lax.dot_general(
                        lhs, rhs, (((0,), (0,)), ((), ())), preferred_element_type=F32
                    )
                    prod = prod[lo_row - h * HALF :, :]
                    old = work[g, base + lo_row : base + hi_row, :]
                    if g == half:
                        col = lax.broadcasted_iota(jnp.int32, old.shape, 1) - offset
                        old = jnp.where((col >= 0) & (col < PANEL), 0.0, old)
                    work[g, base + lo_row : base + hi_row, :] = old - prod


def sketch_kernel(x_ref, s_ref, sk_ref, hi_ref, lo_ref, gram_ref, own_ref):
    x = x_ref[...].astype(F32)
    s = s_ref[...]
    sf = s.astype(F32)
    xsq = jnp.sum(x * x, axis=1, keepdims=True) * (-LOG2E * 4.0 / FEAT)
    ssq = jnp.sum(sf * sf, axis=1, keepdims=True) * (-LOG2E * 4.0 / FEAT)
    x_parts = split3(x * (LOG2E * 8.0 / FEAT))
    xq = split3(xsq)
    sq = split3(ssq)
    lane = lax.broadcasted_iota(jnp.int32, (LEAF, FEAT), 1)
    def tail(parts):
        out = jnp.zeros((LEAF, FEAT), F32)
        for k, part in enumerate(parts):
            out = jnp.where(lane == k, part if isinstance(part,float) else part.astype(F32), out)
        return out.astype(BF16)
    x_tail = tail((*xq, 1.0, 1.0, 1.0))
    s_tail = tail((1.0, 1.0, 1.0, *sq))
    left = jnp.concatenate([x_parts[0], x_parts[1], x_parts[2], x_tail], axis=1)
    right = jnp.concatenate([s, s, s, s_tail], axis=1)
    sk = sk_ref[...]
    gram = jnp.zeros((RANK, 2*RANK), F32)
    for c in range(LEAF//CHUNK):
        z = lax.dot_general(left[c * CHUNK : (c + 1) * CHUNK], right, (((1,), (1,)), ((), ())), preferred_element_type=F32)
        kern = jnp.exp2(z).astype(BF16)
        sketched = jnp.dot(kern, sk, preferred_element_type=F32)
        hi, lo = split2(sketched)
        hi_ref[c * CHUNK : (c + 1) * CHUNK, :] = hi
        lo_ref[c * CHUNK : (c + 1) * CHUNK, :] = lo
        gram += lax.dot_general(hi, jnp.concatenate([hi,lo],axis=1), (((0,), (0,)), ((), ())), preferred_element_type=F32)
    cross=gram[:,RANK:]
    gram=gram[:,:RANK]+cross+cross.T
    gram_ref[...] = gram
    @pl.when(pl.program_id(0) == 0)
    def _():
        own_ref[...] = gram
    @pl.when(pl.program_id(0) != 0)
    def _():
        own_ref[...] += gram


def sketch_all(arranged, samples, sketch):
    rows = arranged.shape[0]
    n = rows // LEAF
    return pl.pallas_call(
        sketch_kernel,
        grid=(n,),
        in_specs=[
            pl.BlockSpec((LEAF, FEAT), lambda i: (i, 0)),
            pl.BlockSpec((LEAF, FEAT), lambda i: (i, 0)),
            pl.BlockSpec((LEAF, RANK), lambda i: (0, 0)),
        ],
        out_specs=[
            pl.BlockSpec((LEAF, RANK), lambda i: (i, 0)),
            pl.BlockSpec((LEAF, RANK), lambda i: (i, 0)),
            pl.BlockSpec((None, RANK, RANK), lambda i: (i, 0, 0)),
            pl.BlockSpec((RANK, RANK), lambda i: (0, 0)),
        ],
        out_shape=[
            jax.ShapeDtypeStruct((rows, RANK), BF16),
            jax.ShapeDtypeStruct((rows, RANK), BF16),
            jax.ShapeDtypeStruct((n, RANK, RANK), F32),
            jax.ShapeDtypeStruct((RANK, RANK), F32),
        ],
        compiler_params=pltpu.CompilerParams(vmem_limit_bytes=48 << 20),
        name="leaf_sketch",
    )(arranged, samples, sketch)

def basis_kernel(gram_ref, hi_ref, lo_ref, out_ref, work, diag, inv_hi, inv_lo):
    @pl.when(pl.program_id(0) == 0)
    def _():
        for m in range(BATCH):
            for h in range(2):
                work[h, m * RANK : (m + 1) * RANK, :] = gram_ref[m, :, h * HALF : (h + 1) * HALF]
        factor_all(work, diag)
        row = lax.broadcasted_iota(jnp.int32, (RANK, HALF), 0)
        col = lax.broadcasted_iota(jnp.int32, (RANK, HALF), 1)
        for m in range(BATCH):
            for h in range(2):
                value = work[h, m * RANK : (m + 1) * RANK, :] * math.sqrt(LEAF)
                value = jnp.where(row >= col + h * HALF, value, 0.0)
                hi, lo = split2(value)
                inv_hi[m, :, h * HALF : (h + 1) * HALF] = hi
                inv_lo[m, :, h * HALF : (h + 1) * HALF] = lo

    leaf = pl.program_id(0)
    dims = (((1,), (1,)), ((), ()))
    ih = inv_hi[leaf]
    il = inv_lo[leaf]
    for c in range(4):
        rows = slice(c * 256, (c + 1) * 256)
        hi = hi_ref[rows, :]
        value = lax.dot_general(hi, ih, dims, preferred_element_type=F32)
        value += lax.dot_general(hi, il, dims, preferred_element_type=F32)
        value += lax.dot_general(lo_ref[rows, :], ih, dims, preferred_element_type=F32)
        out_ref[rows, :] = value.astype(BF16)

def basis_all(grams, hi, lo):
    rows = hi.shape[0]
    n = rows // LEAF
    assert n == BATCH
    return pl.pallas_call(
        basis_kernel,
        grid=(n,),
        in_specs=[
            pl.BlockSpec((n, RANK, RANK), lambda i: (0, 0, 0)),
            pl.BlockSpec((LEAF, RANK), lambda i: (i, 0)),
            pl.BlockSpec((LEAF, RANK), lambda i: (i, 0)),
        ],
        out_specs=pl.BlockSpec((LEAF, RANK), lambda i: (i, 0)),
        out_shape=jax.ShapeDtypeStruct((rows, RANK), BF16),
        scratch_shapes=[
            pltpu.VMEM((2, BATCH * RANK, HALF), F32),
            pltpu.VMEM((BATCH * PANEL, HALF), F32),
            pltpu.VMEM((BATCH, RANK, RANK), BF16),
            pltpu.VMEM((BATCH, RANK, RANK), BF16),
        ],
        compiler_params=pltpu.CompilerParams(vmem_limit_bytes=48 << 20),
        cost_estimate=pl.CostEstimate(flops=16 * 10**9, bytes_accessed=14 * 2**20, transcendentals=0),
        name="leaf_factor",
    )(grams, hi, lo)

def path_kernel(*refs):
    grams, out_ref, work, diag, keep = refs[:-4], refs[-4], refs[-3], refs[-2], refs[-1]
    for m in range(BATCH):
        for h in range(2):
            work[h, m * RANK : (m + 1) * RANK, :] = grams[m][:, h * HALF : (h + 1) * HALF]
    factor_all(work, diag, keep)
    row = lax.broadcasted_iota(jnp.int32, (RANK, HALF), 0)
    col = lax.broadcasted_iota(jnp.int32, (RANK, HALF), 1)
    drow = lax.broadcasted_iota(jnp.int32, (PANEL, HALF), 0)
    dcol = lax.broadcasted_iota(jnp.int32, (PANEL, HALF), 1)
    total = jnp.zeros((RANK, RANK), F32)
    dims = (((1,), (1,)), ((), ()))
    for m in range(BATCH - 1):
        up, inv = [], []
        for h in range(2):
            value = work[h, m * RANK : (m + 1) * RANK, :]
            value = jnp.where(row // PANEL < (col + h * HALF) // PANEL, value, 0.0)
            blocks = []
            for panel in range(RANK // PANEL):
                half, offset = divmod(panel * PANEL, HALF)
                piece = value[panel * PANEL : (panel + 1) * PANEL, :]
                if half == h:
                    block = keep[panel, m * PANEL : (m + 1) * PANEL, :]
                    block = jnp.where((dcol < PANEL) & (drow <= dcol), block, 0.0)
                    if offset:
                        block = pltpu.roll(block, offset, 1)
                    piece = piece + block
                blocks.append(piece)
            up.append(jnp.concatenate(blocks, axis=0))
            value = work[h, (m + 1) * RANK : (m + 2) * RANK, :]
            inv.append(jnp.where(row >= col + h * HALF, value, 0.0))
        uh, ul = split2(jnp.concatenate(up, axis=1))
        ih, il = split2(jnp.concatenate(inv, axis=1))
        total += lax.dot_general(uh, ih, dims, preferred_element_type=F32)
        total += lax.dot_general(uh, il, dims, preferred_element_type=F32)
        total += lax.dot_general(ul, ih, dims, preferred_element_type=F32)
    out_ref[...] = total

def path_all(level_grams):
    assert len(level_grams) == BATCH
    return pl.pallas_call(
        path_kernel,
        out_shape=jax.ShapeDtypeStruct((RANK, RANK), F32),
        scratch_shapes=[
            pltpu.VMEM((2, BATCH * RANK, HALF), F32),
            pltpu.VMEM((BATCH * PANEL, HALF), F32),
            pltpu.VMEM((RANK // PANEL, BATCH * PANEL, HALF), F32),
        ],
        compiler_params=pltpu.CompilerParams(vmem_limit_bytes=48 << 20),
        name="path_factor",
    )(*level_grams)


def swapped(shard, axis, stride):
    return lax.ppermute(shard, axis, [(i, i ^ 1 << stride) for i in range(lax.axis_size(axis))])


def on_device(points, send_order, place_order, sample_rows, sketch):
    count_rows = points.shape[0]
    feature = points.shape[1]
    devices = lax.axis_size(("gx", "gy"))
    peer_rows = count_rows // devices
    outgoing = jnp.take(points, send_order, axis=0)
    incoming = lax.all_to_all(
        outgoing.reshape(devices, peer_rows, feature),
        ("gx", "gy"),
        split_axis=0,
        concat_axis=0,
        tiled=True,
    )
    arranged = jnp.take(incoming.reshape(count_rows, feature), place_order, axis=0)
    requests = sample_rows.reshape(-1, devices)
    picked = jnp.take(
        arranged,
        lax.all_to_all(requests, ("gx", "gy"), split_axis=1, concat_axis=1, tiled=True),
        axis=0,
    )
    samples = lax.all_to_all(picked, ("gx", "gy"), split_axis=1, concat_axis=1, tiled=True).reshape(
        -1, feature
    )
    high, low, grams, own_gram = sketch_all(arranged, samples, sketch)
    levels = devices.bit_length() - 1
    level_grams = [own_gram]
    current = own_gram
    for level in range(levels):
        current = current + swapped(current, ("gx", "gy"), level)
        level_grams.append(current)
    basis = basis_all(grams, high, low)
    path = path_all(level_grams)
    return (basis, path)


def solution(mesh):
    return jax.shard_map(
        on_device,
        mesh=mesh,
        in_specs=(P(("gx", "gy"), None), P(("gx", "gy")), P(("gx", "gy")), P(("gx", "gy")), P()),
        out_specs=(P(("gx", "gy"), None), P(("gx", "gy"), None)),
        check_vma=False,
    )
```

```python
import functools
import math

import jax
import jax.numpy as jnp
from jax import lax
from jax.experimental import pallas as pl
from jax.experimental.pallas import tpu as pltpu
from jax.sharding import PartitionSpec as P

LEAF = 1024
FEAT = 64
RANK = 256
HALF = 128
PANEL = 32
STEP = 8
BATCH = 8
CHUNK = 512
LOG2E = 1.4426950408889634
MB = 1 << 20
F32 = jnp.float32
BF16 = jnp.bfloat16


def split2(x):
    hi = x.astype(BF16)
    return hi, (x - hi.astype(F32)).astype(BF16)


def split3(x):
    hi = x.astype(BF16)
    rest = x - hi.astype(F32)
    mid = rest.astype(BF16)
    return hi, mid, (rest - mid.astype(F32)).astype(BF16)


def eliminate(rows):
    count = len(rows)
    rows = list(rows)
    shape = rows[0].shape

    def lane(row, at):
        return jnp.broadcast_to(row[:, at : at + 1], shape)

    for base in range(0, count, STEP):
        reach = min(2 * STEP, count - base)
        local = rows[base : base + STEP]
        coef = [
            [lane(local[i], base + j) if j >= i else None for j in range(reach)]
            for i in range(STEP)
        ]
        done = []
        for c in range(STEP):
            inv = lax.rsqrt(coef[c][c])
            for j in range(c + 1, reach):
                coef[c][j] = coef[c][j] * inv
            scaled = local[c] * inv
            done.append(scaled)
            for i in range(c + 1, STEP):
                for j in range(i, reach):
                    coef[i][j] = coef[i][j] - coef[c][i] * coef[c][j]
                local[i] = local[i] - coef[c][i] * scaled
        rows[base : base + STEP] = done
        for i in range(base + STEP, count):
            for c in range(STEP):
                factor = coef[c][i - base] if i - base < reach else lane(done[c], i)
                rows[i] = rows[i] - factor * done[c]
    return rows


def factor_all(work, diag, keep=None):
    lanes = lax.broadcasted_iota(jnp.int32, (BATCH, HALF), 1)
    for panel in range(RANK // PANEL):
        start = panel * PANEL
        half, offset = divmod(start, HALF)
        rows = []
        for i in range(PANEL):
            row = work[half, pl.ds(start + i, BATCH, stride=RANK), :]
            if offset:
                row = pltpu.roll(row, HALF - offset, 1)
            unit = jnp.where((lanes & (PANEL - 1)) == i, 1.0, 0.0)
            rows.append(jnp.where(lanes < PANEL, row, unit))
        rows = eliminate(rows)
        for i in range(PANEL):
            diag[pl.ds(i, BATCH, stride=PANEL), :] = rows[i]
        group = lax.broadcasted_iota(jnp.int32, (PANEL, HALF), 1) // PANEL
        in_panel = lax.broadcasted_iota(jnp.int32, (PANEL, HALF), 1) - offset
        at_row = lax.broadcasted_iota(jnp.int32, (PANEL, HALF), 0)
        for m in range(BATCH):
            block = diag[m * PANEL : (m + 1) * PANEL, :]
            if keep is not None:
                keep[panel, m * PANEL : (m + 1) * PANEL, :] = block
            hi, mid, low = split3(block)
            hi, mid, low = (v.astype(F32) for v in (hi, mid, low))
            zero = jnp.zeros_like(hi)
            first = jnp.where(group == 0, zero, hi).astype(BF16)
            second = jnp.where(
                group == 0, zero, jnp.where(group == 3, low, mid)
            ).astype(BF16)
            left = jnp.concatenate([first, second], axis=1)
            base = m * RANK
            fresh = []
            for h in range(2):
                top = work[h, base + start : base + start + PANEL, :]
                if h == half:
                    inside = (in_panel >= 0) & (in_panel < PANEL)
                    top = jnp.where(inside, jnp.where(in_panel == at_row, 1.0, 0.0), top)
                th, tm, tl = split3(top)
                tz = jnp.zeros_like(th)
                right = jnp.concatenate([tz, th, tm, tl, tz, th, tm, th], axis=0)
                new = jnp.dot(left, right, preferred_element_type=F32)
                work[h, base + start : base + start + PANEL, :] = new
                fresh.append(new)
            after = start + PANEL
            if after == RANK:
                continue
            parts = [split3(v) for v in fresh]
            for h in range(2):
                lo_row = max(after, h * HALF)
                hi_row = (h + 1) * HALF
                if lo_row >= hi_row:
                    continue
                ah, am, al = parts[h]
                lhs = jnp.concatenate([ah, ah, am, ah, am, al], axis=0)
                for g in range(2):
                    bh, bm, bl = parts[g]
                    rhs = jnp.concatenate([bh, bm, bh, bl, bm, bh], axis=0)
                    prod = lax.dot_general(
                        lhs, rhs, (((0,), (0,)), ((), ())), preferred_element_type=F32
                    )
                    prod = prod[lo_row - h * HALF :, :]
                    old = work[g, base + lo_row : base + hi_row, :]
                    if g == half:
                        col = lax.broadcasted_iota(jnp.int32, old.shape, 1) - offset
                        old = jnp.where((col >= 0) & (col < PANEL), 0.0, old)
                    work[g, base + lo_row : base + hi_row, :] = old - prod


def duplicate(width, halves):
    row = lax.broadcasted_iota(jnp.int32, (width, HALF * halves), 0)
    col = lax.broadcasted_iota(jnp.int32, (width, HALF * halves), 1)
    return jnp.where(row == (col % FEAT) + FEAT * (col // HALF), 1.0, 0.0).astype(BF16)


def pack_rows(pick, table, packed, blocks, half_rows):
    low = lax.broadcasted_iota(jnp.int32, (1, HALF), 1) < FEAT

    def block(b, carry):
        for q in range(half_rows):
            one = table[pl.ds(pick(b, q), 1), :]
            two = table[pl.ds(pick(b, q + half_rows), 1), :]
            packed[pl.ds(b * half_rows + q, 1), :] = jnp.where(low, one, two)
        return carry

    lax.fori_loop(0, blocks, block, 0)


def emit_packed(packed, out_ref, blocks, half_rows):
    def block(b, carry):
        rows = packed[pl.ds(pl.multiple_of(b * half_rows, half_rows), half_rows), :]
        out_ref[b, 0:half_rows, :] = rows.astype(BF16)
        return carry

    lax.fori_loop(0, blocks, block, 0, unroll=8)


def outgoing_kernel(order_ref, points_ref, rows_ref, out_ref, table, packed, *, blocks, half_rows, extra):
    features, count = points_ref.shape
    spread = duplicate(features, 1)
    piece = 1024

    def build(c, carry):
        at = pl.multiple_of(c * piece, piece)
        table[pl.ds(at, piece), :] = lax.dot_general(
            points_ref[:, pl.ds(at, piece)], spread, (((0,), (0,)), ((), ())), preferred_element_type=F32
        )
        return carry

    lax.fori_loop(0, count // piece, build, 0, unroll=2)
    wanted = rows_ref[...]
    high = (wanted >> 7).astype(F32)
    low = (wanted & 127).astype(F32)
    asked = jnp.concatenate([high, low], axis=0).T
    asked = jnp.concatenate([asked.reshape(blocks, 1, HALF), jnp.zeros((blocks, extra - 1, HALF), F32)], axis=1)
    out_ref[:, half_rows : half_rows + extra, :] = asked.astype(BF16)
    pack_rows(lambda b, q: order_ref[b * 2 * half_rows + q], table, packed, blocks, half_rows)
    emit_packed(packed, out_ref, blocks, half_rows)


def outgoing_rows(points, send_order, sample_rows, blocks):
    count, features = points.shape
    half_rows = count // blocks // 2
    extra = 8
    return pl.pallas_call(
        functools.partial(outgoing_kernel, blocks=blocks, half_rows=half_rows, extra=extra),
        in_specs=[
            pl.BlockSpec(memory_space=pltpu.SMEM),
            pl.BlockSpec(memory_space=pltpu.VMEM),
            pl.BlockSpec(memory_space=pltpu.VMEM),
        ],
        out_shape=jax.ShapeDtypeStruct((blocks, half_rows + extra, HALF), BF16),
        scratch_shapes=[pltpu.VMEM((count, HALF), F32), pltpu.VMEM((count // 2, HALF), F32)],
        compiler_params=pltpu.CompilerParams(vmem_limit_bytes=40 * MB),
        name="outgoing_rows",
    )(send_order, points.T, sample_rows.reshape(-1, blocks))


def build_table(received_ref, table, blocks, half_rows):
    spread = duplicate(HALF, 2)

    def block(b, carry):
        both = jnp.dot(received_ref[b, 0:half_rows, :], spread, preferred_element_type=F32)
        at = pl.multiple_of(b * 2 * half_rows, 2 * half_rows)
        table[pl.ds(at, half_rows), :] = both[:, :HALF]
        table[pl.ds(at + half_rows, half_rows), :] = both[:, HALF:]
        return carry

    lax.fori_loop(0, blocks, block, 0, unroll=16)


def picked_kernel(place_ref, received_ref, out_ref, table, packed, asked, asked_smem, sem, *, blocks, half_rows):
    coded = received_ref[:, half_rows : half_rows + 1, :].astype(F32).reshape(blocks, HALF)
    asked[...] = (coded * 128.0 + pltpu.roll(coded, FEAT, 1)).astype(jnp.int32)
    copy = pltpu.make_async_copy(asked, asked_smem, sem)
    copy.start()
    build_table(received_ref, table, blocks, half_rows)
    copy.wait()
    pack_rows(lambda b, q: place_ref[asked_smem[b, q]], table, packed, blocks, half_rows)
    emit_packed(packed, out_ref, blocks, half_rows)


def picked_rows(received, place_order):
    blocks, padded, _ = received.shape
    count = place_order.shape[0]
    half_rows = count // blocks // 2
    return pl.pallas_call(
        functools.partial(picked_kernel, blocks=blocks, half_rows=half_rows),
        in_specs=[pl.BlockSpec(memory_space=pltpu.SMEM), pl.BlockSpec(memory_space=pltpu.VMEM)],
        out_shape=jax.ShapeDtypeStruct((blocks, half_rows, HALF), BF16),
        scratch_shapes=[
            pltpu.VMEM((count, HALF), F32),
            pltpu.VMEM((count // 2, HALF), F32),
            pltpu.VMEM((blocks, HALF), jnp.int32),
            pltpu.SMEM((blocks, HALF), jnp.int32),
            pltpu.SemaphoreType.DMA,
        ],
        compiler_params=pltpu.CompilerParams(vmem_limit_bytes=40 * MB),
        name="picked_rows",
    )(place_order, received)


def arranged_kernel(place_ref, received_ref, out_ref, table, moved, *, blocks, half_rows):
    build_table(received_ref, table, blocks, half_rows)
    count = out_ref.shape[0]
    piece = 64

    def move(b, carry):
        for q in range(piece):
            moved[pl.ds(b * piece + q, 1), :] = table[pl.ds(place_ref[b * piece + q], 1), :]
        return carry

    lax.fori_loop(0, count // piece, move, 0)
    rows = 128
    lane = lax.broadcasted_iota(jnp.int32, (rows, HALF), 1)

    def prepare(b, carry):
        at = pl.multiple_of(b * rows, rows)
        x = moved[pl.ds(at, rows), :]
        norm = jnp.sum(x * x, axis=1, keepdims=True) * (-LOG2E * 2.0 / FEAT)
        n0, n1, n2 = (v.astype(F32) for v in split3(norm))
        p0, p1, p2 = (v.astype(F32) for v in split3(x * (LOG2E * 8.0 / FEAT)))
        tail = jnp.where(lane == FEAT, n0, jnp.where(lane == FEAT + 1, n1, jnp.where(lane == FEAT + 2, n2, 0.0)))
        out_ref[pl.ds(at, rows), 0:HALF] = jnp.where(lane < FEAT, p0, p1).astype(BF16)
        out_ref[pl.ds(at, rows), HALF : 2 * HALF] = jnp.where(lane < FEAT, p2, tail).astype(BF16)
        return carry

    lax.fori_loop(0, count // rows, prepare, 0)


def arranged_rows(received, place_order):
    blocks, padded, _ = received.shape
    count = place_order.shape[0]
    half_rows = count // blocks // 2
    return pl.pallas_call(
        functools.partial(arranged_kernel, blocks=blocks, half_rows=half_rows),
        in_specs=[pl.BlockSpec(memory_space=pltpu.SMEM), pl.BlockSpec(memory_space=pltpu.VMEM)],
        out_shape=jax.ShapeDtypeStruct((count, 2 * HALF), BF16),
        scratch_shapes=[pltpu.VMEM((count, HALF), F32), pltpu.VMEM((count, HALF), F32)],
        compiler_params=pltpu.CompilerParams(vmem_limit_bytes=40 * MB),
        cost_estimate=pl.CostEstimate(flops=4 * 10**9, bytes_accessed=24 * MB, transcendentals=0),
        name="arranged_rows",
    )(place_order, received)


def sketch_kernel(left_ref, samples_ref, sk_ref, hi_ref, lo_ref, gram_ref, own_ref, wide):
    leaf = pl.program_id(0)
    owners, half_rows, _ = samples_ref.shape
    share = LEAF // owners
    slabs = half_rows // share

    @pl.when(leaf == 0)
    def _():
        wide[...] = samples_ref[...].astype(F32)
        own_ref[...] = jnp.zeros_like(own_ref)

    slab = wide[:, pl.ds(pl.multiple_of((leaf % slabs) * share, share), share), :].reshape(LEAF, HALF).astype(BF16)
    row = lax.broadcasted_iota(jnp.int32, (HALF, HALF), 0)
    col = lax.broadcasted_iota(jnp.int32, (HALF, HALF), 1)
    spread = jnp.where(row == (col % FEAT) + FEAT * (leaf // slabs), 1.0, 0.0).astype(BF16)
    s = jnp.dot(slab, spread, preferred_element_type=F32)
    s_hi, s_lo = split2(s * s)
    first = lax.broadcasted_iota(jnp.int32, (8, HALF), 1) < FEAT
    ones = jnp.where(first, 1.0, 0.0).astype(BF16)
    nt = (((1,), (1,)), ((), ()))
    norm = lax.dot_general(ones, s_hi, nt, preferred_element_type=F32)
    norm += lax.dot_general(ones, s_lo, nt, preferred_element_type=F32)
    norm = norm[0:1, :] * (-LOG2E * 4.0 / FEAT)
    lane = lax.broadcasted_iota(jnp.int32, (LEAF, HALF), 1)
    right = jnp.concatenate([s.astype(BF16), jnp.where(lane < FEAT, s, 1.0).astype(BF16)], axis=1)
    gram = jnp.zeros((RANK, 2 * RANK), F32)
    for c in range(LEAF // CHUNK):
        z = lax.dot_general(left_ref[c * CHUNK : (c + 1) * CHUNK, :], right, nt, preferred_element_type=F32)
        kern = jnp.exp2(z + norm).astype(BF16)
        sketched = jnp.dot(kern, sk_ref[...], preferred_element_type=F32)
        hi, lo = split2(sketched)
        hi_ref[c * CHUNK : (c + 1) * CHUNK, :] = hi
        lo_ref[c * CHUNK : (c + 1) * CHUNK, :] = lo
        gram += lax.dot_general(hi, jnp.concatenate([hi, lo], axis=1), (((0,), (0,)), ((), ())), preferred_element_type=F32)
    cross = gram[:, RANK:]
    gram = gram[:, :RANK] + cross + cross.T
    gram_ref[...] = gram
    own_ref[...] += gram


def sketch_all(left, samples, sketch):
    rows = left.shape[0]
    n = rows // LEAF
    owners, half_rows, _ = samples.shape
    ordered = sketch.reshape(LEAF // owners, owners, RANK).transpose(1, 0, 2).reshape(LEAF, RANK)
    return pl.pallas_call(
        sketch_kernel,
        grid=(n,),
        in_specs=[
            pl.BlockSpec((LEAF, 2 * HALF), lambda i: (i, 0)),
            pl.BlockSpec((owners, half_rows, HALF), lambda i: (0, 0, 0)),
            pl.BlockSpec((LEAF, RANK), lambda i: (0, 0)),
        ],
        out_specs=[
            pl.BlockSpec((LEAF, RANK), lambda i: (i, 0)),
            pl.BlockSpec((LEAF, RANK), lambda i: (i, 0)),
            pl.BlockSpec((None, RANK, RANK), lambda i: (i, 0, 0)),
            pl.BlockSpec((RANK, RANK), lambda i: (0, 0)),
        ],
        out_shape=[
            jax.ShapeDtypeStruct((rows, RANK), BF16),
            jax.ShapeDtypeStruct((rows, RANK), BF16),
            jax.ShapeDtypeStruct((n, RANK, RANK), F32),
            jax.ShapeDtypeStruct((RANK, RANK), F32),
        ],
        scratch_shapes=[pltpu.VMEM((owners, half_rows, HALF), F32)],
        compiler_params=pltpu.CompilerParams(vmem_limit_bytes=48 * MB),
        name="leaf_sketch",
    )(left, samples, ordered)


def basis_kernel(gram_ref, hi_ref, lo_ref, out_ref, work, diag, inv_hi, inv_lo):
    @pl.when(pl.program_id(0) == 0)
    def _():
        for m in range(BATCH):
            for h in range(2):
                work[h, m * RANK : (m + 1) * RANK, :] = gram_ref[m, :, h * HALF : (h + 1) * HALF]
        factor_all(work, diag)
        row = lax.broadcasted_iota(jnp.int32, (RANK, HALF), 0)
        col = lax.broadcasted_iota(jnp.int32, (RANK, HALF), 1)
        for m in range(BATCH):
            for h in range(2):
                value = work[h, m * RANK : (m + 1) * RANK, :] * math.sqrt(LEAF)
                value = jnp.where(row >= col + h * HALF, value, 0.0)
                hi, lo = split2(value)
                inv_hi[m, :, h * HALF : (h + 1) * HALF] = hi
                inv_lo[m, :, h * HALF : (h + 1) * HALF] = lo

    leaf = pl.program_id(0)
    dims = (((1,), (1,)), ((), ()))
    ih = inv_hi[leaf]
    il = inv_lo[leaf]
    for c in range(4):
        rows = slice(c * 256, (c + 1) * 256)
        hi = hi_ref[rows, :]
        value = lax.dot_general(hi, ih, dims, preferred_element_type=F32)
        value += lax.dot_general(hi, il, dims, preferred_element_type=F32)
        value += lax.dot_general(lo_ref[rows, :], ih, dims, preferred_element_type=F32)
        out_ref[rows, :] = value.astype(BF16)

def basis_all(grams, hi, lo):
    rows = hi.shape[0]
    n = rows // LEAF
    assert n == BATCH
    return pl.pallas_call(
        basis_kernel,
        grid=(n,),
        in_specs=[
            pl.BlockSpec((n, RANK, RANK), lambda i: (0, 0, 0)),
            pl.BlockSpec((LEAF, RANK), lambda i: (i, 0)),
            pl.BlockSpec((LEAF, RANK), lambda i: (i, 0)),
        ],
        out_specs=pl.BlockSpec((LEAF, RANK), lambda i: (i, 0)),
        out_shape=jax.ShapeDtypeStruct((rows, RANK), BF16),
        scratch_shapes=[
            pltpu.VMEM((2, BATCH * RANK, HALF), F32),
            pltpu.VMEM((BATCH * PANEL, HALF), F32),
            pltpu.VMEM((BATCH, RANK, RANK), BF16),
            pltpu.VMEM((BATCH, RANK, RANK), BF16),
        ],
        compiler_params=pltpu.CompilerParams(vmem_limit_bytes=48 * MB),
        cost_estimate=pl.CostEstimate(flops=16 * 10**9, bytes_accessed=14 * MB, transcendentals=0),
        name="leaf_factor",
    )(grams, hi, lo)

def path_kernel(*refs):
    grams, out_ref, work, diag, keep = refs[:-4], refs[-4], refs[-3], refs[-2], refs[-1]
    for m in range(BATCH):
        for h in range(2):
            work[h, m * RANK : (m + 1) * RANK, :] = grams[m][:, h * HALF : (h + 1) * HALF]
    factor_all(work, diag, keep)
    row = lax.broadcasted_iota(jnp.int32, (RANK, HALF), 0)
    col = lax.broadcasted_iota(jnp.int32, (RANK, HALF), 1)
    drow = lax.broadcasted_iota(jnp.int32, (PANEL, HALF), 0)
    dcol = lax.broadcasted_iota(jnp.int32, (PANEL, HALF), 1)
    total = jnp.zeros((RANK, RANK), F32)
    dims = (((1,), (1,)), ((), ()))
    for m in range(BATCH - 1):
        up, inv = [], []
        for h in range(2):
            value = work[h, m * RANK : (m + 1) * RANK, :]
            value = jnp.where(row // PANEL < (col + h * HALF) // PANEL, value, 0.0)
            blocks = []
            for panel in range(RANK // PANEL):
                half, offset = divmod(panel * PANEL, HALF)
                piece = value[panel * PANEL : (panel + 1) * PANEL, :]
                if half == h:
                    block = keep[panel, m * PANEL : (m + 1) * PANEL, :]
                    block = jnp.where((dcol < PANEL) & (drow <= dcol), block, 0.0)
                    if offset:
                        block = pltpu.roll(block, offset, 1)
                    piece = piece + block
                blocks.append(piece)
            up.append(jnp.concatenate(blocks, axis=0))
            value = work[h, (m + 1) * RANK : (m + 2) * RANK, :]
            inv.append(jnp.where(row >= col + h * HALF, value, 0.0))
        uh, ul = split2(jnp.concatenate(up, axis=1))
        ih, il = split2(jnp.concatenate(inv, axis=1))
        total += lax.dot_general(uh, ih, dims, preferred_element_type=F32)
        total += lax.dot_general(uh, il, dims, preferred_element_type=F32)
        total += lax.dot_general(ul, ih, dims, preferred_element_type=F32)
    out_ref[...] = total

def path_all(level_grams):
    assert len(level_grams) == BATCH
    return pl.pallas_call(
        path_kernel,
        out_shape=jax.ShapeDtypeStruct((RANK, RANK), F32),
        scratch_shapes=[
            pltpu.VMEM((2, BATCH * RANK, HALF), F32),
            pltpu.VMEM((BATCH * PANEL, HALF), F32),
            pltpu.VMEM((RANK // PANEL, BATCH * PANEL, HALF), F32),
        ],
        compiler_params=pltpu.CompilerParams(vmem_limit_bytes=48 * MB),
        name="path_factor",
    )(*level_grams)


AXES = ("gx", "gy")


def swapped(shard, axis, stride):
    return lax.ppermute(shard, axis, [(i, i ^ 1 << stride) for i in range(lax.axis_size(axis))])


def exchanged(blocks):
    return lax.all_to_all(blocks, AXES, split_axis=0, concat_axis=0, tiled=True)


def on_device(points, send_order, place_order, sample_rows, sketch):
    devices = lax.axis_size(AXES)
    received = exchanged(outgoing_rows(points, send_order, sample_rows, devices))
    samples = exchanged(picked_rows(received, place_order))
    left = arranged_rows(received, place_order)
    high, low, grams, own_gram = sketch_all(left, samples, sketch)
    levels = devices.bit_length() - 1
    level_grams = [own_gram]
    current = own_gram
    for level in range(levels):
        current = current + swapped(current, AXES, level)
        level_grams.append(current)
    basis = basis_all(grams, high, low)
    path = path_all(level_grams)
    return (basis, path)


def solution(mesh):
    return jax.shard_map(
        on_device,
        mesh=mesh,
        in_specs=(P(AXES, None), P(AXES), P(AXES), P(AXES), P()),
        out_specs=(P(AXES, None), P(AXES, None)),
        check_vma=False,
    )
```

```python
import functools
import math

import jax
import jax.numpy as jnp
from jax import lax
from jax.experimental import pallas as pl
from jax.experimental.pallas import tpu as pltpu
from jax.sharding import PartitionSpec as P

LEAF = 1024
FEAT = 64
RANK = 256
HALF = 128
PANEL = 32
STEP = 8
BATCH = 8
SPLIT = 4
CHUNK = 512
LOG2E = 1.4426950408889634
MB = 1 << 20
F32 = jnp.float32
BF16 = jnp.bfloat16


def split2(x):
    hi = x.astype(BF16)
    return hi, (x - hi.astype(F32)).astype(BF16)


def split3(x):
    hi = x.astype(BF16)
    rest = x - hi.astype(F32)
    mid = rest.astype(BF16)
    return hi, mid, (rest - mid.astype(F32)).astype(BF16)


def eliminate(rows):
    count = len(rows)
    rows = list(rows)
    shape = rows[0].shape

    def lane(row, at):
        return jnp.broadcast_to(row[:, at : at + 1], shape)

    for base in range(0, count, STEP):
        reach = min(2 * STEP, count - base)
        local = rows[base : base + STEP]
        coef = [
            [lane(local[i], base + j) if j >= i else None for j in range(reach)]
            for i in range(STEP)
        ]
        done = []
        for c in range(STEP):
            inv = lax.rsqrt(coef[c][c])
            for j in range(c + 1, reach):
                coef[c][j] = coef[c][j] * inv
            scaled = local[c] * inv
            done.append(scaled)
            for i in range(c + 1, STEP):
                for j in range(i, reach):
                    coef[i][j] = coef[i][j] - coef[c][i] * coef[c][j]
                local[i] = local[i] - coef[c][i] * scaled
        rows[base : base + STEP] = done
        for i in range(base + STEP, count):
            for c in range(STEP):
                factor = coef[c][i - base] if i - base < reach else lane(done[c], i)
                rows[i] = rows[i] - factor * done[c]
    return rows


def factor_all(work, diag, keep=None, first=0, last=RANK // PANEL):
    lanes = lax.broadcasted_iota(jnp.int32, (BATCH, HALF), 1)
    for panel in range(first, last):
        start = panel * PANEL
        half, offset = divmod(start, HALF)
        rows = []
        for i in range(PANEL):
            row = work[half, pl.ds(start + i, BATCH, stride=RANK), :]
            if offset:
                row = pltpu.roll(row, HALF - offset, 1)
            unit = jnp.where((lanes & (PANEL - 1)) == i, 1.0, 0.0)
            rows.append(jnp.where(lanes < PANEL, row, unit))
        rows = eliminate(rows)
        for i in range(PANEL):
            diag[pl.ds(i, BATCH, stride=PANEL), :] = rows[i]
        group = lax.broadcasted_iota(jnp.int32, (PANEL, HALF), 1) // PANEL
        in_panel = lax.broadcasted_iota(jnp.int32, (PANEL, HALF), 1) - offset
        at_row = lax.broadcasted_iota(jnp.int32, (PANEL, HALF), 0)
        for m in range(BATCH):
            block = diag[m * PANEL : (m + 1) * PANEL, :]
            if keep is not None:
                keep[panel, m * PANEL : (m + 1) * PANEL, :] = block
            hi, mid, low = split3(block)
            hi, mid, low = (v.astype(F32) for v in (hi, mid, low))
            zero = jnp.zeros_like(hi)
            left_hi = jnp.where(group == 0, zero, hi).astype(BF16)
            left_lo = jnp.where(
                group == 0, zero, jnp.where(group == 3, low, mid)
            ).astype(BF16)
            left = jnp.concatenate([left_hi, left_lo], axis=1)
            base = m * RANK
            fresh = []
            for h in range(2):
                top = work[h, base + start : base + start + PANEL, :]
                if h == half:
                    inside = (in_panel >= 0) & (in_panel < PANEL)
                    top = jnp.where(inside, jnp.where(in_panel == at_row, 1.0, 0.0), top)
                th, tm, tl = split3(top)
                tz = jnp.zeros_like(th)
                right = jnp.concatenate([tz, th, tm, tl, tz, th, tm, th], axis=0)
                new = jnp.dot(left, right, preferred_element_type=F32)
                work[h, base + start : base + start + PANEL, :] = new
                fresh.append(new)
            after = start + PANEL
            if after == RANK:
                continue
            parts = [split3(v) for v in fresh]
            for h in range(2):
                lo_row = max(after, h * HALF)
                hi_row = (h + 1) * HALF
                if lo_row >= hi_row:
                    continue
                ah, am, al = parts[h]
                lhs = jnp.concatenate([ah, ah, am, ah, am, al], axis=0)
                for g in range(2):
                    bh, bm, bl = parts[g]
                    rhs = jnp.concatenate([bh, bm, bh, bl, bm, bh], axis=0)
                    prod = lax.dot_general(
                        lhs, rhs, (((0,), (0,)), ((), ())), preferred_element_type=F32
                    )
                    prod = prod[lo_row - h * HALF :, :]
                    old = work[g, base + lo_row : base + hi_row, :]
                    if g == half:
                        col = lax.broadcasted_iota(jnp.int32, old.shape, 1) - offset
                        old = jnp.where((col >= 0) & (col < PANEL), 0.0, old)
                    work[g, base + lo_row : base + hi_row, :] = old - prod


def duplicate(width, halves):
    row = lax.broadcasted_iota(jnp.int32, (width, HALF * halves), 0)
    col = lax.broadcasted_iota(jnp.int32, (width, HALF * halves), 1)
    return jnp.where(row == (col % FEAT) + FEAT * (col // HALF), 1.0, 0.0).astype(BF16)


def pack_rows(pick, table, packed, blocks, half_rows):
    low = lax.broadcasted_iota(jnp.int32, (1, HALF), 1) < FEAT

    def block(b, carry):
        for q in range(half_rows):
            one = table[pl.ds(pick(b, q), 1), :]
            two = table[pl.ds(pick(b, q + half_rows), 1), :]
            packed[pl.ds(b * half_rows + q, 1), :] = jnp.where(low, one, two)
        return carry

    lax.fori_loop(0, blocks, block, 0)


def emit_packed(packed, out_ref, blocks, half_rows):
    def block(b, carry):
        rows = packed[pl.ds(pl.multiple_of(b * half_rows, half_rows), half_rows), :]
        out_ref[b, 0:half_rows, :] = rows.astype(BF16)
        return carry

    lax.fori_loop(0, blocks, block, 0, unroll=8)


def outgoing_kernel(order_ref, points_ref, rows_ref, out_ref, table, packed, *, blocks, half_rows, extra):
    features, count = points_ref.shape
    spread = duplicate(features, 1)
    piece = 1024

    def build(c, carry):
        at = pl.multiple_of(c * piece, piece)
        table[pl.ds(at, piece), :] = lax.dot_general(
            points_ref[:, pl.ds(at, piece)], spread, (((0,), (0,)), ((), ())), preferred_element_type=F32
        )
        return carry

    lax.fori_loop(0, count // piece, build, 0, unroll=2)
    wanted = rows_ref[...]
    high = (wanted >> 7).astype(F32)
    low = (wanted & 127).astype(F32)
    asked = jnp.concatenate([high, low], axis=0).T
    asked = jnp.concatenate([asked.reshape(blocks, 1, HALF), jnp.zeros((blocks, extra - 1, HALF), F32)], axis=1)
    out_ref[:, half_rows : half_rows + extra, :] = asked.astype(BF16)
    pack_rows(lambda b, q: order_ref[b * 2 * half_rows + q], table, packed, blocks, half_rows)
    emit_packed(packed, out_ref, blocks, half_rows)


def outgoing_rows(points, send_order, sample_rows, blocks):
    count, features = points.shape
    half_rows = count // blocks // 2
    extra = 8
    return pl.pallas_call(
        functools.partial(outgoing_kernel, blocks=blocks, half_rows=half_rows, extra=extra),
        in_specs=[
            pl.BlockSpec(memory_space=pltpu.SMEM),
            pl.BlockSpec(memory_space=pltpu.VMEM),
            pl.BlockSpec(memory_space=pltpu.VMEM),
        ],
        out_shape=jax.ShapeDtypeStruct((blocks, half_rows + extra, HALF), BF16),
        scratch_shapes=[pltpu.VMEM((count, HALF), F32), pltpu.VMEM((count // 2, HALF), F32)],
        compiler_params=pltpu.CompilerParams(vmem_limit_bytes=16 * MB),
        name="outgoing_rows",
    )(send_order, points.T, sample_rows.reshape(-1, blocks))


def build_table(received_ref, table, blocks, half_rows):
    spread = duplicate(HALF, 2)

    def block(b, carry):
        both = jnp.dot(received_ref[b, 0:half_rows, :], spread, preferred_element_type=F32)
        at = pl.multiple_of(b * 2 * half_rows, 2 * half_rows)
        table[pl.ds(at, half_rows), :] = both[:, :HALF]
        table[pl.ds(at + half_rows, half_rows), :] = both[:, HALF:]
        return carry

    lax.fori_loop(0, blocks, block, 0, unroll=16)


def picked_kernel(place_ref, received_ref, out_ref, table, packed, asked, asked_smem, sem, *, blocks, half_rows):
    coded = received_ref[:, half_rows : half_rows + 1, :].astype(F32).reshape(blocks, HALF)
    asked[...] = (coded * 128.0 + pltpu.roll(coded, FEAT, 1)).astype(jnp.int32)
    copy = pltpu.make_async_copy(asked, asked_smem, sem)
    copy.start()
    build_table(received_ref, table, blocks, half_rows)
    copy.wait()
    pack_rows(lambda b, q: place_ref[asked_smem[b, q]], table, packed, blocks, half_rows)
    emit_packed(packed, out_ref, blocks, half_rows)


def picked_rows(received, place_order):
    blocks, padded, _ = received.shape
    count = place_order.shape[0]
    half_rows = count // blocks // 2
    return pl.pallas_call(
        functools.partial(picked_kernel, blocks=blocks, half_rows=half_rows),
        in_specs=[pl.BlockSpec(memory_space=pltpu.SMEM), pl.BlockSpec(memory_space=pltpu.VMEM)],
        out_shape=jax.ShapeDtypeStruct((blocks, half_rows, HALF), BF16),
        scratch_shapes=[
            pltpu.VMEM((count, HALF), F32),
            pltpu.VMEM((count // 2, HALF), F32),
            pltpu.VMEM((blocks, HALF), jnp.int32),
            pltpu.SMEM((blocks, HALF), jnp.int32),
            pltpu.SemaphoreType.DMA,
        ],
        compiler_params=pltpu.CompilerParams(vmem_limit_bytes=16 * MB),
        name="picked_rows",
    )(place_order, received)


def arranged_kernel(place_ref, received_ref, out_ref, table, moved, *, blocks, half_rows):
    build_table(received_ref, table, blocks, half_rows)
    count = out_ref.shape[0]
    piece = 64

    def move(b, carry):
        for q in range(piece):
            moved[pl.ds(b * piece + q, 1), :] = table[pl.ds(place_ref[b * piece + q], 1), :]
        return carry

    lax.fori_loop(0, count // piece, move, 0)
    rows = 128
    lane = lax.broadcasted_iota(jnp.int32, (rows, HALF), 1)

    def prepare(b, carry):
        at = pl.multiple_of(b * rows, rows)
        x = moved[pl.ds(at, rows), :]
        norm = jnp.sum(x * x, axis=1, keepdims=True) * (-LOG2E * 2.0 / FEAT)
        n0, n1, n2 = (v.astype(F32) for v in split3(norm))
        p0, p1, p2 = (v.astype(F32) for v in split3(x * (LOG2E * 8.0 / FEAT)))
        tail = jnp.where(lane == FEAT, n0, jnp.where(lane == FEAT + 1, n1, jnp.where(lane == FEAT + 2, n2, 0.0)))
        out_ref[pl.ds(at, rows), 0:HALF] = jnp.where(lane < FEAT, p0, p1).astype(BF16)
        out_ref[pl.ds(at, rows), HALF : 2 * HALF] = jnp.where(lane < FEAT, p2, tail).astype(BF16)
        return carry

    lax.fori_loop(0, count // rows, prepare, 0)


def arranged_rows(received, place_order):
    blocks, padded, _ = received.shape
    count = place_order.shape[0]
    half_rows = count // blocks // 2
    return pl.pallas_call(
        functools.partial(arranged_kernel, blocks=blocks, half_rows=half_rows),
        in_specs=[pl.BlockSpec(memory_space=pltpu.SMEM), pl.BlockSpec(memory_space=pltpu.VMEM)],
        out_shape=jax.ShapeDtypeStruct((count, 2 * HALF), BF16),
        scratch_shapes=[pltpu.VMEM((count, HALF), F32), pltpu.VMEM((count, HALF), F32)],
        compiler_params=pltpu.CompilerParams(vmem_limit_bytes=20 * MB),
        cost_estimate=pl.CostEstimate(flops=4 * 10**9, bytes_accessed=24 * MB, transcendentals=0),
        name="arranged_rows",
    )(place_order, received)


def sketch_kernel(left_ref, samples_ref, sk_ref, hi_ref, lo_ref, gram_ref, own_ref, wide, own):
    leaf = pl.program_id(0)
    owners, half_rows, _ = samples_ref.shape
    share = LEAF // owners
    slabs = half_rows // share

    @pl.when(leaf == 0)
    def _():
        wide[...] = samples_ref[...].astype(F32)
        own[...] = jnp.zeros_like(own)

    slab = wide[:, pl.ds(pl.multiple_of((leaf % slabs) * share, share), share), :].reshape(LEAF, HALF).astype(BF16)
    row = lax.broadcasted_iota(jnp.int32, (HALF, HALF), 0)
    col = lax.broadcasted_iota(jnp.int32, (HALF, HALF), 1)
    spread = jnp.where(row == (col % FEAT) + FEAT * (leaf // slabs), 1.0, 0.0).astype(BF16)
    s = jnp.dot(slab, spread, preferred_element_type=F32)
    s_hi, s_lo = split2(s * s)
    first = lax.broadcasted_iota(jnp.int32, (8, HALF), 1) < FEAT
    ones = jnp.where(first, 1.0, 0.0).astype(BF16)
    nt = (((1,), (1,)), ((), ()))
    norm = lax.dot_general(ones, s_hi, nt, preferred_element_type=F32)
    norm += lax.dot_general(ones, s_lo, nt, preferred_element_type=F32)
    norm = norm[0:1, :] * (-LOG2E * 4.0 / FEAT)
    lane = lax.broadcasted_iota(jnp.int32, (LEAF, HALF), 1)
    right = jnp.concatenate([s.astype(BF16), jnp.where(lane < FEAT, s, 1.0).astype(BF16)], axis=1)
    gram = jnp.zeros((RANK, 2 * RANK), F32)
    for c in range(LEAF // CHUNK):
        z = lax.dot_general(left_ref[c * CHUNK : (c + 1) * CHUNK, :], right, nt, preferred_element_type=F32)
        kern = jnp.exp2(z + norm).astype(BF16)
        sketched = jnp.dot(kern, sk_ref[...], preferred_element_type=F32)
        hi, lo = split2(sketched)
        hi_ref[c * CHUNK : (c + 1) * CHUNK, :] = hi
        lo_ref[c * CHUNK : (c + 1) * CHUNK, :] = lo
        gram += lax.dot_general(hi, jnp.concatenate([hi, lo], axis=1), (((0,), (0,)), ((), ())), preferred_element_type=F32)
    cross = gram[:, RANK:]
    gram = gram[:, :RANK] + cross + cross.T
    gram_ref[...] = gram
    own[...] += gram

    @pl.when(leaf == pl.num_programs(0) - 1)
    def _():
        cross_part, both, diagonal = pack_symmetric(own[...])
        own_ref[0:HALF, :] = cross_part
        own_ref[HALF : 2 * HALF, :] = both
        own_ref[2 * HALF : 2 * HALF + 8, :] = diagonal


def sketch_all(left, samples, sketch):
    rows = left.shape[0]
    n = rows // LEAF
    owners, half_rows, _ = samples.shape
    ordered = sketch.reshape(LEAF // owners, owners, RANK).transpose(1, 0, 2).reshape(LEAF, RANK)
    return pl.pallas_call(
        sketch_kernel,
        grid=(n,),
        in_specs=[
            pl.BlockSpec((LEAF, 2 * HALF), lambda i: (i, 0)),
            pl.BlockSpec((owners, half_rows, HALF), lambda i: (0, 0, 0)),
            pl.BlockSpec((LEAF, RANK), lambda i: (0, 0)),
        ],
        out_specs=[
            pl.BlockSpec((LEAF, RANK), lambda i: (i, 0)),
            pl.BlockSpec((LEAF, RANK), lambda i: (i, 0)),
            pl.BlockSpec((None, RANK, RANK), lambda i: (i, 0, 0)),
            pl.BlockSpec((2 * HALF + 8, HALF), lambda i: (0, 0)),
        ],
        out_shape=[
            jax.ShapeDtypeStruct((rows, RANK), BF16),
            jax.ShapeDtypeStruct((rows, RANK), BF16),
            jax.ShapeDtypeStruct((n, RANK, RANK), F32),
            jax.ShapeDtypeStruct((2 * HALF + 8, HALF), F32),
        ],
        scratch_shapes=[pltpu.VMEM((owners, half_rows, HALF), F32), pltpu.VMEM((RANK, RANK), F32)],
        compiler_params=pltpu.CompilerParams(vmem_limit_bytes=28 * MB),
        name="leaf_sketch",
    )(left, samples, ordered)


def load_grams(gram_ref, work):
    for m in range(BATCH):
        for h in range(2):
            work[h, m * RANK : (m + 1) * RANK, :] = gram_ref[m, :, h * HALF : (h + 1) * HALF]


def begin_kernel(gram_ref, work, diag):
    load_grams(gram_ref, work)
    factor_all(work, diag, last=SPLIT)


def begin_factor(grams):
    return pl.pallas_call(
        begin_kernel,
        out_shape=jax.ShapeDtypeStruct((2, BATCH * RANK, HALF), F32),
        scratch_shapes=[pltpu.VMEM((BATCH * PANEL, HALF), F32)],
        compiler_params=pltpu.CompilerParams(vmem_limit_bytes=14 * MB),
        cost_estimate=pl.CostEstimate(flops=14 * 10**9, bytes_accessed=4 * MB, transcendentals=0),
        name="begin_factor",
    )(grams)


def basis_kernel(state_ref, hi_ref, lo_ref, out_ref, work, diag, inv_hi, inv_lo):
    @pl.when(pl.program_id(0) == 0)
    def _():
        work[...] = state_ref[...]
        factor_all(work, diag, first=SPLIT)
        row = lax.broadcasted_iota(jnp.int32, (RANK, HALF), 0)
        col = lax.broadcasted_iota(jnp.int32, (RANK, HALF), 1)
        for m in range(BATCH):
            for h in range(2):
                value = work[h, m * RANK : (m + 1) * RANK, :] * math.sqrt(LEAF)
                value = jnp.where(row >= col + h * HALF, value, 0.0)
                hi, lo = split2(value)
                inv_hi[m, :, h * HALF : (h + 1) * HALF] = hi
                inv_lo[m, :, h * HALF : (h + 1) * HALF] = lo

    leaf = pl.program_id(0)
    dims = (((1,), (1,)), ((), ()))
    ih = inv_hi[leaf]
    il = inv_lo[leaf]
    for c in range(4):
        rows = slice(c * 256, (c + 1) * 256)
        hi = hi_ref[rows, :]
        value = lax.dot_general(hi, ih, dims, preferred_element_type=F32)
        value += lax.dot_general(hi, il, dims, preferred_element_type=F32)
        value += lax.dot_general(lo_ref[rows, :], ih, dims, preferred_element_type=F32)
        out_ref[rows, :] = value.astype(BF16)


def basis_all(state, hi, lo):
    rows = hi.shape[0]
    n = rows // LEAF
    assert n == BATCH
    return pl.pallas_call(
        basis_kernel,
        grid=(n,),
        in_specs=[
            pl.BlockSpec((2, BATCH * RANK, HALF), lambda i: (0, 0, 0)),
            pl.BlockSpec((LEAF, RANK), lambda i: (i, 0)),
            pl.BlockSpec((LEAF, RANK), lambda i: (i, 0)),
        ],
        out_specs=pl.BlockSpec((LEAF, RANK), lambda i: (i, 0)),
        out_shape=jax.ShapeDtypeStruct((rows, RANK), BF16),
        scratch_shapes=[
            pltpu.VMEM((2, BATCH * RANK, HALF), F32),
            pltpu.VMEM((BATCH * PANEL, HALF), F32),
            pltpu.VMEM((BATCH, RANK, RANK), BF16),
            pltpu.VMEM((BATCH, RANK, RANK), BF16),
        ],
        compiler_params=pltpu.CompilerParams(vmem_limit_bytes=24 * MB),
        cost_estimate=pl.CostEstimate(flops=20 * 10**9, bytes_accessed=14 * MB, transcendentals=0),
        name="leaf_factor",
    )(state, hi, lo)


def pack_symmetric(gram):
    row = lax.broadcasted_iota(jnp.int32, (HALF, HALF), 0)
    col = lax.broadcasted_iota(jnp.int32, (HALF, HALF), 1)
    first = gram[:HALF, :HALF]
    last = gram[HALF:, HALF:]
    diagonal = jnp.sum(jnp.where(row == col, first, 0.0), axis=0, keepdims=True)
    return gram[:HALF, HALF:], jnp.where(row > col, first, last), jnp.broadcast_to(diagonal, (8, HALF))


def unpack_symmetric(packed):
    row = lax.broadcasted_iota(jnp.int32, (HALF, HALF), 0)
    col = lax.broadcasted_iota(jnp.int32, (HALF, HALF), 1)
    cross = packed[:HALF]
    both = packed[HALF : 2 * HALF]
    below = jnp.where(row > col, both, 0.0)
    above = jnp.where(row < col, both, 0.0)
    first = below + below.T + jnp.where(row == col, packed[2 * HALF : 2 * HALF + 1], 0.0)
    last = above + above.T + jnp.where(row == col, both, 0.0)
    return first, cross, last


def level_sums(place, gathered, current, levels):
    sums = []
    for level in range(levels):
        sibling = ((place >> level) ^ 1) << level
        for j in range(1 << level):
            current = current + gathered[sibling + j]
        sums.append(current)
    return sums


def path_kernel(where_ref, lower_ref, upper_ref, out_ref, work, diag, keep):
    near = where_ref[0]
    far = where_ref[1]
    own = lower_ref[near]
    packed = [own] + level_sums(near, lower_ref, own, 3)
    packed += level_sums(far, upper_ref, upper_ref[far], 4)
    for m in range(BATCH):
        first, cross, last = unpack_symmetric(packed[m])
        base = m * RANK
        work[0, base : base + HALF, :] = first
        work[1, base : base + HALF, :] = cross
        work[0, base + HALF : base + RANK, :] = cross.T
        work[1, base + HALF : base + RANK, :] = last
    factor_all(work, diag, keep)
    row = lax.broadcasted_iota(jnp.int32, (RANK, HALF), 0)
    col = lax.broadcasted_iota(jnp.int32, (RANK, HALF), 1)
    drow = lax.broadcasted_iota(jnp.int32, (PANEL, HALF), 0)
    dcol = lax.broadcasted_iota(jnp.int32, (PANEL, HALF), 1)
    total = jnp.zeros((RANK, RANK), F32)
    dims = (((1,), (1,)), ((), ()))
    for m in range(BATCH - 1):
        up, inv = [], []
        for h in range(2):
            value = work[h, m * RANK : (m + 1) * RANK, :]
            value = jnp.where(row // PANEL < (col + h * HALF) // PANEL, value, 0.0)
            blocks = []
            for panel in range(RANK // PANEL):
                half, offset = divmod(panel * PANEL, HALF)
                piece = value[panel * PANEL : (panel + 1) * PANEL, :]
                if half == h:
                    block = keep[panel, m * PANEL : (m + 1) * PANEL, :]
                    block = jnp.where((dcol < PANEL) & (drow <= dcol), block, 0.0)
                    if offset:
                        block = pltpu.roll(block, offset, 1)
                    piece = piece + block
                blocks.append(piece)
            up.append(jnp.concatenate(blocks, axis=0))
            value = work[h, (m + 1) * RANK : (m + 2) * RANK, :]
            inv.append(jnp.where(row >= col + h * HALF, value, 0.0))
        uh, ul = split2(jnp.concatenate(up, axis=1))
        ih, il = split2(jnp.concatenate(inv, axis=1))
        total += lax.dot_general(uh, ih, dims, preferred_element_type=F32)
        total += lax.dot_general(uh, il, dims, preferred_element_type=F32)
        total += lax.dot_general(ul, ih, dims, preferred_element_type=F32)
    out_ref[...] = total

def path_all(where, lower, upper):
    return pl.pallas_call(
        path_kernel,
        in_specs=[
            pl.BlockSpec(memory_space=pltpu.SMEM),
            pl.BlockSpec(memory_space=pltpu.VMEM),
            pl.BlockSpec(memory_space=pltpu.VMEM),
        ],
        out_shape=jax.ShapeDtypeStruct((RANK, RANK), F32),
        scratch_shapes=[
            pltpu.VMEM((2, BATCH * RANK, HALF), F32),
            pltpu.VMEM((BATCH * PANEL, HALF), F32),
            pltpu.VMEM((RANK // PANEL, BATCH * PANEL, HALF), F32),
        ],
        compiler_params=pltpu.CompilerParams(vmem_limit_bytes=24 * MB),
        name="path_factor",
    )(where, lower, upper)


AXES = ("gx", "gy")


def exchanged(blocks):
    return lax.all_to_all(blocks, AXES, split_axis=0, concat_axis=0, tiled=True)


def on_device(points, send_order, place_order, sample_rows, sketch):
    devices = lax.axis_size(AXES)
    received = exchanged(outgoing_rows(points, send_order, sample_rows, devices))
    samples = exchanged(picked_rows(received, place_order))
    left = arranged_rows(received, place_order)
    high, low, grams, own_gram = sketch_all(left, samples, sketch)
    lower = lax.all_gather(own_gram, "gy")
    state = begin_factor(grams)
    shared = jnp.sum(lower, axis=0)
    state, shared = lax.optimization_barrier((state, shared))
    upper = lax.all_gather(shared, "gx")
    basis = basis_all(state, high, low)
    place = jnp.stack([lax.axis_index("gy"), lax.axis_index("gx")]).astype(jnp.int32)
    path = path_all(place, lower, upper)
    return (basis, path)


def solution(mesh):
    return jax.shard_map(
        on_device,
        mesh=mesh,
        in_specs=(P(AXES, None), P(AXES), P(AXES), P(AXES), P()),
        out_specs=(P(AXES, None), P(AXES, None)),
        check_vma=False,
    )
```

```python
import functools
import math

import jax
import jax.numpy as jnp
from jax import lax
from jax.experimental import pallas as pl
from jax.experimental.pallas import tpu as pltpu
from jax.sharding import PartitionSpec as P

LEAF = 1024
FEAT = 64
RANK = 256
HALF = 128
PANEL = 32
STEP = 8
BATCH = 8
FIRST_CUT = 3
SECOND_CUT = 6
CHUNK = 512
LOG2E = 1.4426950408889634
MB = 1 << 20
F32 = jnp.float32
BF16 = jnp.bfloat16


def split2(x):
    hi = x.astype(BF16)
    return hi, (x - hi.astype(F32)).astype(BF16)


def split3(x):
    hi = x.astype(BF16)
    rest = x - hi.astype(F32)
    mid = rest.astype(BF16)
    return hi, mid, (rest - mid.astype(F32)).astype(BF16)


def eliminate(rows):
    count = len(rows)
    shape = rows[0].shape

    def lane(row, at):
        return jnp.broadcast_to(row[:, at : at + 1], shape)

    for base in range(0, count, STEP):
        reach = min(2 * STEP, count - base)
        local = rows[base : base + STEP]
        coef = [
            [lane(local[i], base + j) if j >= i else None for j in range(reach)]
            for i in range(STEP)
        ]
        done = []
        for c in range(STEP):
            inv = lax.rsqrt(coef[c][c])
            for j in range(c + 1, reach):
                coef[c][j] = coef[c][j] * inv
            scaled = local[c] * inv
            done.append(scaled)
            for i in range(c + 1, STEP):
                for j in range(i, reach):
                    coef[i][j] = coef[i][j] - coef[c][i] * coef[c][j]
                local[i] = local[i] - coef[c][i] * scaled
        rows[base : base + STEP] = done
        for i in range(base + STEP, count):
            for c in range(STEP):
                factor = coef[c][i - base] if i - base < reach else lane(done[c], i)
                rows[i] = rows[i] - factor * done[c]
        yield


def factor_all(work, diag, keep=None, first=0, last=RANK // PANEL):
    lanes = lax.broadcasted_iota(jnp.int32, (BATCH, HALF), 1)
    waiting = []

    def update(m, start, parts, low_row, high_row):
        half, offset = divmod(start, HALF)
        base = m * RANK
        left, rights = parts
        left = left[low_row - start - PANEL : high_row - start - PANEL]
        for g in range(2):
            prod = jnp.dot(left, rights[g], preferred_element_type=F32)
            old = work[g, base + low_row : base + high_row, :]
            if g == half:
                col = lax.broadcasted_iota(jnp.int32, old.shape, 1) - offset
                old = jnp.where((col >= 0) & (col < PANEL), 0.0, old)
            work[g, base + low_row : base + high_row, :] = old - prod

    def unit_rows(begin):
        row = lax.broadcasted_iota(jnp.int32, (RANK - begin, RANK), 0)
        col = lax.broadcasted_iota(jnp.int32, (RANK - begin, RANK), 1)
        return jnp.where(row + begin == col, 1.0, 0.0).astype(BF16)

    for panel in range(first, last):
        start = panel * PANEL
        half, offset = divmod(start, HALF)
        rows = []
        for i in range(PANEL):
            row = work[half, pl.ds(start + i, BATCH, stride=RANK), :]
            if offset:
                row = pltpu.roll(row, HALF - offset, 1)
            unit = jnp.where((lanes & (PANEL - 1)) == i, 1.0, 0.0)
            rows.append(jnp.where(lanes < PANEL, row, unit))
        groups = PANEL // STEP
        for step, _ in enumerate(eliminate(rows)):
            share = -(-len(waiting) // (groups - step))
            for args in waiting[:share]:
                update(*args)
            waiting = waiting[share:]
        for i in range(PANEL):
            diag[pl.ds(i, BATCH, stride=PANEL), :] = rows[i]
        group = lax.broadcasted_iota(jnp.int32, (PANEL, HALF), 1) // PANEL
        in_panel = lax.broadcasted_iota(jnp.int32, (PANEL, HALF), 1) - offset
        at_row = lax.broadcasted_iota(jnp.int32, (PANEL, HALF), 0)
        after = start + PANEL
        fresh = []
        for m in range(BATCH):
            block = diag[m * PANEL : (m + 1) * PANEL, :]
            if keep is not None:
                keep[panel, m * PANEL : (m + 1) * PANEL, :] = block
            hi, mid, low = split3(block)
            hi, mid, low = (v.astype(F32) for v in (hi, mid, low))
            zero = jnp.zeros_like(hi)
            left_hi = jnp.where(group == 0, zero, hi).astype(BF16)
            left_lo = jnp.where(group == 0, zero, jnp.where(group == 3, low, mid)).astype(BF16)
            left = jnp.concatenate([left_hi, left_lo], axis=1)
            base = m * RANK
            parts = []
            for h in range(2):
                top = work[h, base + start : base + start + PANEL, :]
                if h == half:
                    inside = (in_panel >= 0) & (in_panel < PANEL)
                    top = jnp.where(inside, jnp.where(in_panel == at_row, 1.0, 0.0), top)
                th, tm, tl = split3(top)
                tz = jnp.zeros_like(th)
                right = jnp.concatenate([tz, th, tm, tl, tz, th, tm, th], axis=0)
                new = jnp.dot(left, right, preferred_element_type=F32)
                work[h, base + start : base + start + PANEL, :] = new
                parts.append(split3(new))
            if after < RANK:
                stack = [
                    jnp.concatenate([h_, h_, m_, h_, m_, l_], axis=0) for h_, m_, l_ in parts
                ]
                mirror = lax.dot_general(
                    unit_rows(after), jnp.concatenate(stack, axis=1), (((1,), (1,)), ((), ())), preferred_element_type=F32
                )
                rights = [jnp.concatenate([h_, m_, h_, l_, m_, h_], axis=0) for h_, m_, l_ in parts]
                fresh.append((mirror.astype(BF16), rights))
        if after == RANK:
            continue
        for m in range(BATCH):
            update(m, start, fresh[m], after, after + PANEL)
        for m in range(BATCH):
            for h in range(2):
                low_row = max(after + PANEL, h * HALF)
                if low_row < (h + 1) * HALF:
                    waiting.append((m, start, fresh[m], low_row, (h + 1) * HALF))
        if panel == last - 1:
            for args in waiting:
                update(*args)


def duplicate(width, halves):
    row = lax.broadcasted_iota(jnp.int32, (width, HALF * halves), 0)
    col = lax.broadcasted_iota(jnp.int32, (width, HALF * halves), 1)
    return jnp.where(row == (col % FEAT) + FEAT * (col // HALF), 1.0, 0.0).astype(BF16)


def pack_rows(pick, table, packed, blocks, half_rows):
    low = lax.broadcasted_iota(jnp.int32, (1, HALF), 1) < FEAT

    def block(b, carry):
        for q in range(half_rows):
            one = table[pl.ds(pick(b, q), 1), :]
            two = table[pl.ds(pick(b, q + half_rows), 1), :]
            packed[pl.ds(b * half_rows + q, 1), :] = jnp.where(low, one, two)
        return carry

    lax.fori_loop(0, blocks, block, 0)


def emit_packed(packed, out_ref, blocks, half_rows):
    def block(b, carry):
        rows = packed[pl.ds(pl.multiple_of(b * half_rows, half_rows), half_rows), :]
        out_ref[b, 0:half_rows, :] = rows.astype(BF16)
        return carry

    lax.fori_loop(0, blocks, block, 0, unroll=8)


def outgoing_kernel(order_ref, points_ref, rows_ref, out_ref, table, packed, *, blocks, half_rows, extra):
    features, count = points_ref.shape
    spread = duplicate(features, 1)
    piece = 1024

    def build(c, carry):
        at = pl.multiple_of(c * piece, piece)
        table[pl.ds(at, piece), :] = lax.dot_general(
            points_ref[:, pl.ds(at, piece)], spread, (((0,), (0,)), ((), ())), preferred_element_type=F32
        )
        return carry

    lax.fori_loop(0, count // piece, build, 0, unroll=2)
    wanted = rows_ref[...]
    high = (wanted >> 7).astype(F32)
    low = (wanted & 127).astype(F32)
    asked = jnp.concatenate([high, low], axis=0).T
    asked = jnp.concatenate([asked.reshape(blocks, 1, HALF), jnp.zeros((blocks, extra - 1, HALF), F32)], axis=1)
    out_ref[:, half_rows : half_rows + extra, :] = asked.astype(BF16)
    pack_rows(lambda b, q: order_ref[b * 2 * half_rows + q], table, packed, blocks, half_rows)
    emit_packed(packed, out_ref, blocks, half_rows)


def outgoing_rows(points, send_order, sample_rows, blocks):
    count, features = points.shape
    half_rows = count // blocks // 2
    extra = 8
    return pl.pallas_call(
        functools.partial(outgoing_kernel, blocks=blocks, half_rows=half_rows, extra=extra),
        in_specs=[
            pl.BlockSpec(memory_space=pltpu.SMEM),
            pl.BlockSpec(memory_space=pltpu.VMEM),
            pl.BlockSpec(memory_space=pltpu.VMEM),
        ],
        out_shape=jax.ShapeDtypeStruct((blocks, half_rows + extra, HALF), BF16),
        scratch_shapes=[pltpu.VMEM((count, HALF), F32), pltpu.VMEM((count // 2, HALF), F32)],
        compiler_params=pltpu.CompilerParams(vmem_limit_bytes=16 * MB),
        name="outgoing_rows",
    )(send_order, points.T, sample_rows.reshape(-1, blocks))


def build_table(received_ref, table, blocks, half_rows):
    spread = duplicate(HALF, 2)

    def block(b, carry):
        both = jnp.dot(received_ref[b, 0:half_rows, :], spread, preferred_element_type=F32)
        at = pl.multiple_of(b * 2 * half_rows, 2 * half_rows)
        table[pl.ds(at, half_rows), :] = both[:, :HALF]
        table[pl.ds(at + half_rows, half_rows), :] = both[:, HALF:]
        return carry

    lax.fori_loop(0, blocks, block, 0, unroll=16)


def picked_kernel(place_ref, received_ref, out_ref, table, packed, asked, asked_smem, sem, *, blocks, half_rows):
    coded = received_ref[:, half_rows : half_rows + 1, :].astype(F32).reshape(blocks, HALF)
    asked[...] = (coded * 128.0 + pltpu.roll(coded, FEAT, 1)).astype(jnp.int32)
    copy = pltpu.make_async_copy(asked, asked_smem, sem)
    copy.start()
    build_table(received_ref, table, blocks, half_rows)
    copy.wait()
    pack_rows(lambda b, q: place_ref[asked_smem[b, q]], table, packed, blocks, half_rows)
    emit_packed(packed, out_ref, blocks, half_rows)


def picked_rows(received, place_order):
    blocks, padded, _ = received.shape
    count = place_order.shape[0]
    half_rows = count // blocks // 2
    return pl.pallas_call(
        functools.partial(picked_kernel, blocks=blocks, half_rows=half_rows),
        in_specs=[pl.BlockSpec(memory_space=pltpu.SMEM), pl.BlockSpec(memory_space=pltpu.VMEM)],
        out_shape=jax.ShapeDtypeStruct((blocks, half_rows, HALF), BF16),
        scratch_shapes=[
            pltpu.VMEM((count, HALF), F32),
            pltpu.VMEM((count // 2, HALF), F32),
            pltpu.VMEM((blocks, HALF), jnp.int32),
            pltpu.SMEM((blocks, HALF), jnp.int32),
            pltpu.SemaphoreType.DMA,
        ],
        compiler_params=pltpu.CompilerParams(vmem_limit_bytes=16 * MB),
        name="picked_rows",
    )(place_order, received)


def arranged_kernel(place_ref, received_ref, out_ref, table, moved, *, blocks, half_rows):
    build_table(received_ref, table, blocks, half_rows)
    count = out_ref.shape[0]
    piece = 64

    def move(b, carry):
        for q in range(piece):
            moved[pl.ds(b * piece + q, 1), :] = table[pl.ds(place_ref[b * piece + q], 1), :]
        return carry

    lax.fori_loop(0, count // piece, move, 0)
    rows = 128
    lane = lax.broadcasted_iota(jnp.int32, (rows, HALF), 1)

    def prepare(b, carry):
        at = pl.multiple_of(b * rows, rows)
        x = moved[pl.ds(at, rows), :]
        norm = jnp.sum(x * x, axis=1, keepdims=True) * (-LOG2E * 2.0 / FEAT)
        n0, n1, n2 = (v.astype(F32) for v in split3(norm))
        p0, p1, p2 = (v.astype(F32) for v in split3(x * (LOG2E * 8.0 / FEAT)))
        tail = jnp.where(lane == FEAT, n0, jnp.where(lane == FEAT + 1, n1, jnp.where(lane == FEAT + 2, n2, 0.0)))
        out_ref[pl.ds(at, rows), 0:HALF] = jnp.where(lane < FEAT, p0, p1).astype(BF16)
        out_ref[pl.ds(at, rows), HALF : 2 * HALF] = jnp.where(lane < FEAT, p2, tail).astype(BF16)
        return carry

    lax.fori_loop(0, count // rows, prepare, 0)


def arranged_rows(received, place_order):
    blocks, padded, _ = received.shape
    count = place_order.shape[0]
    half_rows = count // blocks // 2
    return pl.pallas_call(
        functools.partial(arranged_kernel, blocks=blocks, half_rows=half_rows),
        in_specs=[pl.BlockSpec(memory_space=pltpu.SMEM), pl.BlockSpec(memory_space=pltpu.VMEM)],
        out_shape=jax.ShapeDtypeStruct((count, 2 * HALF), BF16),
        scratch_shapes=[pltpu.VMEM((count, HALF), F32), pltpu.VMEM((count, HALF), F32)],
        compiler_params=pltpu.CompilerParams(vmem_limit_bytes=58 * MB),
        cost_estimate=pl.CostEstimate(flops=4 * 10**9, bytes_accessed=24 * MB, transcendentals=0),
        name="arranged_rows",
    )(place_order, received)


def sketch_kernel(left_ref, samples_ref, sk_ref, hi_ref, lo_ref, gram_ref, own_ref, wide, own):
    leaf = pl.program_id(0)
    owners, half_rows, _ = samples_ref.shape
    share = LEAF // owners
    slabs = half_rows // share

    @pl.when(leaf == 0)
    def _():
        wide[...] = samples_ref[...].astype(F32)
        own[...] = jnp.zeros_like(own)

    slab = wide[:, pl.ds(pl.multiple_of((leaf % slabs) * share, share), share), :].reshape(LEAF, HALF).astype(BF16)
    row = lax.broadcasted_iota(jnp.int32, (HALF, HALF), 0)
    col = lax.broadcasted_iota(jnp.int32, (HALF, HALF), 1)
    spread = jnp.where(row == (col % FEAT) + FEAT * (leaf // slabs), 1.0, 0.0).astype(BF16)
    s = jnp.dot(slab, spread, preferred_element_type=F32)
    s_hi, s_lo = split2(s * s)
    first = lax.broadcasted_iota(jnp.int32, (8, HALF), 1) < FEAT
    ones = jnp.where(first, 1.0, 0.0).astype(BF16)
    nt = (((1,), (1,)), ((), ()))
    norm = lax.dot_general(ones, s_hi, nt, preferred_element_type=F32)
    norm += lax.dot_general(ones, s_lo, nt, preferred_element_type=F32)
    norm = norm[0:1, :] * (-LOG2E * 4.0 / FEAT)
    lane = lax.broadcasted_iota(jnp.int32, (LEAF, HALF), 1)
    right = jnp.concatenate([s.astype(BF16), jnp.where(lane < FEAT, s, 1.0).astype(BF16)], axis=1)
    gram = jnp.zeros((RANK, 2 * RANK), F32)
    for c in range(LEAF // CHUNK):
        z = lax.dot_general(left_ref[c * CHUNK : (c + 1) * CHUNK, :], right, nt, preferred_element_type=F32)
        kern = jnp.exp2(z + norm).astype(BF16)
        sketched = jnp.dot(kern, sk_ref[...], preferred_element_type=F32)
        hi, lo = split2(sketched)
        hi_ref[c * CHUNK : (c + 1) * CHUNK, :] = hi
        lo_ref[c * CHUNK : (c + 1) * CHUNK, :] = lo
        gram += lax.dot_general(hi, jnp.concatenate([hi, lo], axis=1), (((0,), (0,)), ((), ())), preferred_element_type=F32)
    cross = gram[:, RANK:]
    gram = gram[:, :RANK] + cross + cross.T
    gram_ref[...] = gram
    own[...] += gram

    @pl.when(leaf == pl.num_programs(0) - 1)
    def _():
        cross_part, both, diagonal = pack_symmetric(own[...])
        own_ref[0:HALF, :] = cross_part
        own_ref[HALF : 2 * HALF, :] = both
        own_ref[2 * HALF : 2 * HALF + 8, :] = diagonal


def sketch_all(left, samples, sketch):
    rows = left.shape[0]
    n = rows // LEAF
    owners, half_rows, _ = samples.shape
    ordered = sketch.reshape(LEAF // owners, owners, RANK).transpose(1, 0, 2).reshape(LEAF, RANK)
    return pl.pallas_call(
        sketch_kernel,
        grid=(n,),
        in_specs=[
            pl.BlockSpec((LEAF, 2 * HALF), lambda i: (i, 0)),
            pl.BlockSpec((owners, half_rows, HALF), lambda i: (0, 0, 0)),
            pl.BlockSpec((LEAF, RANK), lambda i: (0, 0)),
        ],
        out_specs=[
            pl.BlockSpec((LEAF, RANK), lambda i: (i, 0)),
            pl.BlockSpec((LEAF, RANK), lambda i: (i, 0)),
            pl.BlockSpec((None, RANK, RANK), lambda i: (i, 0, 0)),
            pl.BlockSpec((2 * HALF + 8, HALF), lambda i: (0, 0)),
        ],
        out_shape=[
            jax.ShapeDtypeStruct((rows, RANK), BF16),
            jax.ShapeDtypeStruct((rows, RANK), BF16),
            jax.ShapeDtypeStruct((n, RANK, RANK), F32),
            jax.ShapeDtypeStruct((2 * HALF + 8, HALF), F32),
        ],
        scratch_shapes=[pltpu.VMEM((owners, half_rows, HALF), F32), pltpu.VMEM((RANK, RANK), F32)],
        compiler_params=pltpu.CompilerParams(vmem_limit_bytes=52 * MB),
        name="leaf_sketch",
    )(left, samples, ordered)


def load_grams(gram_ref, work):
    for m in range(BATCH):
        for h in range(2):
            work[h, m * RANK : (m + 1) * RANK, :] = gram_ref[m, :, h * HALF : (h + 1) * HALF]


def begin_kernel(gram_ref, work, diag):
    load_grams(gram_ref, work)
    factor_all(work, diag, last=FIRST_CUT)


def middle_kernel(state_ref, work, diag):
    work[...] = state_ref[...]
    factor_all(work, diag, first=FIRST_CUT, last=SECOND_CUT)


def factor_part(kernel, name, operand):
    return pl.pallas_call(
        kernel,
        out_shape=jax.ShapeDtypeStruct((2, BATCH * RANK, HALF), F32),
        scratch_shapes=[pltpu.VMEM((BATCH * PANEL, HALF), F32)],
        compiler_params=pltpu.CompilerParams(vmem_limit_bytes=24 * MB),
        cost_estimate=pl.CostEstimate(flops=8 * 10**9, bytes_accessed=4 * MB, transcendentals=0),
        name=name,
    )(operand)


def basis_kernel(state_ref, hi_ref, lo_ref, out_ref, work, diag, inv_hi, inv_lo):
    @pl.when(pl.program_id(0) == 0)
    def _():
        work[...] = state_ref[...]
        factor_all(work, diag, first=SECOND_CUT)
        row = lax.broadcasted_iota(jnp.int32, (RANK, HALF), 0)
        col = lax.broadcasted_iota(jnp.int32, (RANK, HALF), 1)
        for m in range(BATCH):
            for h in range(2):
                value = work[h, m * RANK : (m + 1) * RANK, :] * math.sqrt(LEAF)
                value = jnp.where(row >= col + h * HALF, value, 0.0)
                hi, lo = split2(value)
                inv_hi[m, :, h * HALF : (h + 1) * HALF] = hi
                inv_lo[m, :, h * HALF : (h + 1) * HALF] = lo

    leaf = pl.program_id(0)
    dims = (((1,), (1,)), ((), ()))
    ih = inv_hi[leaf]
    il = inv_lo[leaf]
    for c in range(4):
        rows = slice(c * 256, (c + 1) * 256)
        hi = hi_ref[rows, :]
        value = lax.dot_general(hi, ih, dims, preferred_element_type=F32)
        value += lax.dot_general(hi, il, dims, preferred_element_type=F32)
        value += lax.dot_general(lo_ref[rows, :], ih, dims, preferred_element_type=F32)
        out_ref[rows, :] = value.astype(BF16)


def basis_all(state, hi, lo):
    rows = hi.shape[0]
    n = rows // LEAF
    assert n == BATCH
    return pl.pallas_call(
        basis_kernel,
        grid=(n,),
        in_specs=[
            pl.BlockSpec((2, BATCH * RANK, HALF), lambda i: (0, 0, 0)),
            pl.BlockSpec((LEAF, RANK), lambda i: (i, 0)),
            pl.BlockSpec((LEAF, RANK), lambda i: (i, 0)),
        ],
        out_specs=pl.BlockSpec((LEAF, RANK), lambda i: (i, 0)),
        out_shape=jax.ShapeDtypeStruct((rows, RANK), BF16),
        scratch_shapes=[
            pltpu.VMEM((2, BATCH * RANK, HALF), F32),
            pltpu.VMEM((BATCH * PANEL, HALF), F32),
            pltpu.VMEM((BATCH, RANK, RANK), BF16),
            pltpu.VMEM((BATCH, RANK, RANK), BF16),
        ],
        compiler_params=pltpu.CompilerParams(vmem_limit_bytes=48 * MB),
        cost_estimate=pl.CostEstimate(flops=10 * 10**9, bytes_accessed=14 * MB, transcendentals=0),
        name="leaf_factor",
    )(state, hi, lo)


def pack_symmetric(gram):
    row = lax.broadcasted_iota(jnp.int32, (HALF, HALF), 0)
    col = lax.broadcasted_iota(jnp.int32, (HALF, HALF), 1)
    first = gram[:HALF, :HALF]
    last = gram[HALF:, HALF:]
    diagonal = jnp.sum(jnp.where(row == col, first, 0.0), axis=0, keepdims=True)
    return gram[:HALF, HALF:], jnp.where(row > col, first, last), jnp.broadcast_to(diagonal, (8, HALF))


def unpack_symmetric(packed):
    row = lax.broadcasted_iota(jnp.int32, (HALF, HALF), 0)
    col = lax.broadcasted_iota(jnp.int32, (HALF, HALF), 1)
    cross = packed[:HALF]
    both = packed[HALF : 2 * HALF]
    below = jnp.where(row > col, both, 0.0)
    above = jnp.where(row < col, both, 0.0)
    first = below + below.T + jnp.where(row == col, packed[2 * HALF : 2 * HALF + 1], 0.0)
    last = above + above.T + jnp.where(row == col, both, 0.0)
    return first, cross, last


def path_kernel(
    own_ref, pair_ref, near_ref, chips_ref, row_ref, plane_ref, one_ref, two_ref, three_ref, out_ref, work, diag, keep
):
    packed = [own_ref[...], pair_ref[...], pair_ref[...] + near_ref[...], chips_ref[...]]
    packed += [chips_ref[...] + row_ref[...], plane_ref[...]]
    packed.append(plane_ref[...] + one_ref[...])
    packed.append(packed[-1] + (two_ref[...] + three_ref[...]))
    for m in range(BATCH):
        first, cross, last = unpack_symmetric(packed[m])
        base = m * RANK
        work[0, base : base + HALF, :] = first
        work[1, base : base + HALF, :] = cross
        work[0, base + HALF : base + RANK, :] = cross.T
        work[1, base + HALF : base + RANK, :] = last
    factor_all(work, diag, keep)
    row = lax.broadcasted_iota(jnp.int32, (RANK, HALF), 0)
    col = lax.broadcasted_iota(jnp.int32, (RANK, HALF), 1)
    drow = lax.broadcasted_iota(jnp.int32, (PANEL, HALF), 0)
    dcol = lax.broadcasted_iota(jnp.int32, (PANEL, HALF), 1)
    total = jnp.zeros((RANK, RANK), F32)
    dims = (((1,), (1,)), ((), ()))
    for m in range(BATCH - 1):
        up, inv = [], []
        for h in range(2):
            value = work[h, m * RANK : (m + 1) * RANK, :]
            value = jnp.where(row // PANEL < (col + h * HALF) // PANEL, value, 0.0)
            blocks = []
            for panel in range(RANK // PANEL):
                half, offset = divmod(panel * PANEL, HALF)
                piece = value[panel * PANEL : (panel + 1) * PANEL, :]
                if half == h:
                    block = keep[panel, m * PANEL : (m + 1) * PANEL, :]
                    block = jnp.where((dcol < PANEL) & (drow <= dcol), block, 0.0)
                    if offset:
                        block = pltpu.roll(block, offset, 1)
                    piece = piece + block
                blocks.append(piece)
            up.append(jnp.concatenate(blocks, axis=0))
            value = work[h, (m + 1) * RANK : (m + 2) * RANK, :]
            inv.append(jnp.where(row >= col + h * HALF, value, 0.0))
        uh, ul = split2(jnp.concatenate(up, axis=1))
        ih, il = split2(jnp.concatenate(inv, axis=1))
        total += lax.dot_general(uh, ih, dims, preferred_element_type=F32)
        total += lax.dot_general(uh, il, dims, preferred_element_type=F32)
        total += lax.dot_general(ul, ih, dims, preferred_element_type=F32)
    out_ref[...] = total

def path_all(*packed):
    return pl.pallas_call(
        path_kernel,
        out_shape=jax.ShapeDtypeStruct((RANK, RANK), F32),
        scratch_shapes=[
            pltpu.VMEM((2, BATCH * RANK, HALF), F32),
            pltpu.VMEM((BATCH * PANEL, HALF), F32),
            pltpu.VMEM((RANK // PANEL, BATCH * PANEL, HALF), F32),
        ],
        compiler_params=pltpu.CompilerParams(vmem_limit_bytes=24 * MB),
        name="path_factor",
    )(*packed)


AXES = ("gx", "gy")


def partner(shard, axis, step):
    return lax.ppermute(shard, axis, [(i, i ^ step) for i in range(lax.axis_size(axis))])


def exchanged(blocks):
    return lax.all_to_all(blocks, AXES, split_axis=0, concat_axis=0, tiled=True)


def on_device(points, send_order, place_order, sample_rows, sketch):
    devices = lax.axis_size(AXES)
    received = exchanged(outgoing_rows(points, send_order, sample_rows, devices))
    samples = exchanged(picked_rows(received, place_order))
    left = arranged_rows(received, place_order)
    high, low, grams, own_gram = sketch_all(left, samples, sketch)
    pair = own_gram + partner(own_gram, "gy", 1)
    grams, pair = lax.optimization_barrier((grams, pair))
    near = [partner(pair, "gy", step) for step in (2, 4, 6)]
    state = factor_part(begin_kernel, "begin_factor", grams)
    chips = pair + near[0] + (near[1] + near[2])
    state, chips = lax.optimization_barrier((state, chips))
    rows = [partner(chips, "gx", step) for step in (1, 2, 3)]
    state = factor_part(middle_kernel, "middle_factor", state)
    plane = chips + rows[0] + (rows[1] + rows[2])
    state, plane = lax.optimization_barrier((state, plane))
    far = [partner(plane, "gx", step) for step in (4, 8, 12)]
    basis = basis_all(state, high, low)
    path = path_all(own_gram, pair, near[0], chips, rows[0], plane, *far)
    return (basis, path)


def solution(mesh):
    return jax.shard_map(
        on_device,
        mesh=mesh,
        in_specs=(P(AXES, None), P(AXES), P(AXES), P(AXES), P()),
        out_specs=(P(AXES, None), P(AXES, None)),
        check_vma=False,
    )
```

```python
import functools
import math

import jax
import jax.numpy as jnp
from jax import lax
from jax.experimental import pallas as pl
from jax.experimental.pallas import tpu as pltpu
from jax.sharding import PartitionSpec as P

LEAF = 1024
FEAT = 64
RANK = 256
HALF = 128
PANEL = 32
STEP = 8
BATCH = 8
FIRST_CUT = 3
SECOND_CUT = 6
CHUNK = 1024
LOG2E = 1.4426950408889634
MB = 1 << 20
F32 = jnp.float32
BF16 = jnp.bfloat16


def split2(x):
    hi = x.astype(BF16)
    return hi, (x - hi.astype(F32)).astype(BF16)


def split3(x):
    hi = x.astype(BF16)
    rest = x - hi.astype(F32)
    mid = rest.astype(BF16)
    return hi, mid, (rest - mid.astype(F32)).astype(BF16)


def eliminate(rows, half, offset):
    count = len(rows)
    shape = rows[0][0].shape
    lanes = lax.broadcasted_iota(jnp.int32, shape, 1) - offset

    def lane(row, at):
        return jnp.broadcast_to(row[half][:, offset + at : offset + at + 1], shape)

    def subtract(row, factor, pivot):
        return [row[h] - factor * pivot[h] for h in range(2)]

    for base in range(0, count, STEP):
        reach = min(2 * STEP, count - base)
        local = rows[base : base + STEP]
        coef = [
            [lane(local[i], base + j) if j >= i else None for j in range(reach)]
            for i in range(STEP)
        ]
        done = []
        lower = []
        for c in range(STEP):
            inv = lax.rsqrt(coef[c][c])
            for j in range(c + 1, reach):
                coef[c][j] = coef[c][j] * inv
            scaled = [local[c][h] * inv for h in range(2)]
            scaled[half] = jnp.where(lanes == base + c, inv, scaled[half])
            done.append(scaled)
            for i in range(c + 1, STEP):
                for j in range(i, reach):
                    coef[i][j] = coef[i][j] - coef[c][i] * coef[c][j]
                row = list(local[i])
                row[half] = jnp.where(lanes == base + c, 0.0, row[half])
                local[i] = subtract(row, coef[c][i], scaled)
            keep = list(scaled)
            keep[half] = jnp.where((lanes > base + c) & (lanes < base + STEP), 0.0, scaled[half])
            lower.append(keep)
        rows[base : base + STEP] = done
        for i in range(base + STEP, count):
            row = list(rows[i])
            row[half] = jnp.where((lanes >= base) & (lanes < base + STEP), 0.0, row[half])
            for c in range(STEP):
                factor = coef[c][i - base] if i - base < reach else lane(done[c], i)
                row = subtract(row, factor, lower[c])
            rows[i] = row
        yield


def factor_all(work, first=0, last=RANK // PANEL):
    waiting = []

    def unit_rows(begin):
        row = lax.broadcasted_iota(jnp.int32, (RANK - begin, RANK), 0)
        col = lax.broadcasted_iota(jnp.int32, (RANK - begin, RANK), 1)
        return jnp.where(row + begin == col, 1.0, 0.0).astype(BF16)

    def update(m, start, parts, low_row, high_row):
        half, offset = divmod(start, HALF)
        base = m * RANK
        left, rights = parts
        left = left[low_row - start - PANEL : high_row - start - PANEL]
        for g in range(2):
            prod = jnp.dot(left, rights[g], preferred_element_type=F32)
            old = work[g, base + low_row : base + high_row, :]
            if g == half:
                col = lax.broadcasted_iota(jnp.int32, old.shape, 1) - offset
                old = jnp.where((col >= 0) & (col < PANEL), 0.0, old)
            work[g, base + low_row : base + high_row, :] = old - prod

    for panel in range(first, last):
        start = panel * PANEL
        half, offset = divmod(start, HALF)
        rows = [[work[h, pl.ds(start + i, BATCH, stride=RANK), :] for h in range(2)] for i in range(PANEL)]
        groups = PANEL // STEP
        for step, _ in enumerate(eliminate(rows, half, offset)):
            share = -(-len(waiting) // (groups - step))
            for args in waiting[:share]:
                update(*args)
            waiting = waiting[share:]
        for i in range(PANEL):
            for h in range(2):
                work[h, pl.ds(start + i, BATCH, stride=RANK), :] = rows[i][h]
        after = start + PANEL
        if after == RANK:
            break
        col = lax.broadcasted_iota(jnp.int32, (PANEL, HALF), 1) - offset
        row = lax.broadcasted_iota(jnp.int32, (PANEL, HALF), 0)
        beyond = (col > row) & (col < PANEL)
        fresh = []
        for m in range(BATCH):
            parts = []
            for h in range(2):
                top = work[h, m * RANK + start : m * RANK + after, :]
                parts.append(split3(jnp.where(beyond, 0.0, top) if h == half else top))
            stack = [jnp.concatenate([hi, hi, mid, hi, mid, low], axis=0) for hi, mid, low in parts]
            mirror = lax.dot_general(
                unit_rows(after),
                jnp.concatenate(stack, axis=1),
                (((1,), (1,)), ((), ())),
                preferred_element_type=F32,
            )
            rights = [jnp.concatenate([hi, mid, hi, low, mid, hi], axis=0) for hi, mid, low in parts]
            fresh.append((mirror.astype(BF16), rights))
        for m in range(BATCH):
            update(m, start, fresh[m], after, after + PANEL)
        for m in range(BATCH):
            for h in range(2):
                low_row = max(after + PANEL, h * HALF)
                if low_row < (h + 1) * HALF:
                    waiting.append((m, start, fresh[m], low_row, (h + 1) * HALF))
        if panel == last - 1:
            for args in waiting:
                update(*args)


def duplicate(width, halves):
    row = lax.broadcasted_iota(jnp.int32, (width, HALF * halves), 0)
    col = lax.broadcasted_iota(jnp.int32, (width, HALF * halves), 1)
    return jnp.where(row == (col % FEAT) + FEAT * (col // HALF), 1.0, 0.0).astype(BF16)


def pack_rows(pick, table, packed, blocks, half_rows):
    low = lax.broadcasted_iota(jnp.int32, (1, HALF), 1) < FEAT

    def block(b, carry):
        for q in range(half_rows):
            one = table[pl.ds(pick(b, q), 1), :]
            two = table[pl.ds(pick(b, q + half_rows), 1), :]
            packed[pl.ds(b * half_rows + q, 1), :] = jnp.where(low, one, two)
        return carry

    lax.fori_loop(0, blocks, block, 0)


def emit_packed(packed, out_ref, blocks, half_rows):
    def block(b, carry):
        rows = packed[pl.ds(pl.multiple_of(b * half_rows, half_rows), half_rows), :]
        out_ref[b, 0:half_rows, :] = rows.astype(BF16)
        return carry

    lax.fori_loop(0, blocks, block, 0, unroll=8)


def outgoing_kernel(
    order_hbm, points_hbm, rows_hbm, out_ref, order_ref, points_ref, rows_ref, sem, table, packed, *, blocks, half_rows, extra
):
    features, count = points_ref.shape
    pairs = ((points_hbm, points_ref), (rows_hbm, rows_ref), (order_hbm, order_ref))
    copies = [pltpu.make_async_copy(src, dst, sem.at[k]) for k, (src, dst) in enumerate(pairs)]
    for copy in copies:
        copy.start()
    copies[0].wait()
    spread = duplicate(features, 1)
    piece = 1024

    def build(c, carry):
        at = pl.multiple_of(c * piece, piece)
        table[pl.ds(at, piece), :] = lax.dot_general(
            points_ref[:, pl.ds(at, piece)], spread, (((0,), (0,)), ((), ())), preferred_element_type=F32
        )
        return carry

    lax.fori_loop(0, count // piece, build, 0, unroll=2)
    copies[1].wait()
    wanted = rows_ref[...]
    high = (wanted >> 7).astype(F32)
    low = (wanted & 127).astype(F32)
    asked = jnp.concatenate([high, low], axis=0).T
    asked = jnp.concatenate([asked.reshape(blocks, 1, HALF), jnp.zeros((blocks, extra - 1, HALF), F32)], axis=1)
    out_ref[:, half_rows : half_rows + extra, :] = asked.astype(BF16)
    copies[2].wait()
    pack_rows(lambda b, q: order_ref[b * 2 * half_rows + q], table, packed, blocks, half_rows)
    emit_packed(packed, out_ref, blocks, half_rows)


def outgoing_rows(points, send_order, sample_rows, blocks):
    count, features = points.shape
    half_rows = count // blocks // 2
    extra = 8
    return pl.pallas_call(
        functools.partial(outgoing_kernel, blocks=blocks, half_rows=half_rows, extra=extra),
        in_specs=[pl.BlockSpec(memory_space=pl.ANY)] * 3,
        out_shape=jax.ShapeDtypeStruct((blocks, half_rows + extra, HALF), BF16),
        scratch_shapes=[
            pltpu.SMEM((count,), jnp.int32),
            pltpu.VMEM((features, count), BF16),
            pltpu.VMEM((count // blocks, blocks), jnp.int32),
            pltpu.SemaphoreType.DMA((3,)),
            pltpu.VMEM((count, HALF), F32),
            pltpu.VMEM((count // 2, HALF), F32),
        ],
        compiler_params=pltpu.CompilerParams(vmem_limit_bytes=58 * MB),
        name="outgoing_rows",
    )(send_order, points.T, sample_rows.reshape(-1, blocks))


def build_table(received_ref, table, blocks, half_rows):
    spread = duplicate(HALF, 2)

    def block(b, carry):
        both = jnp.dot(received_ref[b, 0:half_rows, :], spread, preferred_element_type=F32)
        at = pl.multiple_of(b * 2 * half_rows, 2 * half_rows)
        table[pl.ds(at, half_rows), :] = both[:, :HALF]
        table[pl.ds(at + half_rows, half_rows), :] = both[:, HALF:]
        return carry

    lax.fori_loop(0, blocks, block, 0, unroll=16)


def picked_kernel(place_ref, received_ref, out_ref, table, packed, asked, asked_smem, sem, *, blocks, half_rows):
    coded = received_ref[:, half_rows : half_rows + 1, :].astype(F32).reshape(blocks, HALF)
    asked[...] = (coded * 128.0 + pltpu.roll(coded, FEAT, 1)).astype(jnp.int32)
    copy = pltpu.make_async_copy(asked, asked_smem, sem)
    copy.start()
    build_table(received_ref, table, blocks, half_rows)
    copy.wait()
    pack_rows(lambda b, q: place_ref[asked_smem[b, q]], table, packed, blocks, half_rows)
    emit_packed(packed, out_ref, blocks, half_rows)


def picked_rows(received, place_order):
    blocks, padded, _ = received.shape
    count = place_order.shape[0]
    half_rows = count // blocks // 2
    return pl.pallas_call(
        functools.partial(picked_kernel, blocks=blocks, half_rows=half_rows),
        in_specs=[pl.BlockSpec(memory_space=pltpu.SMEM), pl.BlockSpec(memory_space=pltpu.VMEM)],
        out_shape=jax.ShapeDtypeStruct((blocks, half_rows, HALF), BF16),
        scratch_shapes=[
            pltpu.VMEM((count, HALF), F32),
            pltpu.VMEM((count // 2, HALF), F32),
            pltpu.VMEM((blocks, HALF), jnp.int32),
            pltpu.SMEM((blocks, HALF), jnp.int32),
            pltpu.SemaphoreType.DMA,
        ],
        compiler_params=pltpu.CompilerParams(vmem_limit_bytes=16 * MB),
        name="picked_rows",
    )(place_order, received)


def arranged_kernel(place_ref, received_ref, out_ref, table, moved, *, blocks, half_rows):
    build_table(received_ref, table, blocks, half_rows)
    count = out_ref.shape[0]
    piece = 64

    def move(b, carry):
        for q in range(piece):
            moved[pl.ds(b * piece + q, 1), :] = table[pl.ds(place_ref[b * piece + q], 1), :]
        return carry

    lax.fori_loop(0, count // piece, move, 0)
    rows = 128
    lane = lax.broadcasted_iota(jnp.int32, (rows, HALF), 1)

    def prepare(b, carry):
        at = pl.multiple_of(b * rows, rows)
        x = moved[pl.ds(at, rows), :]
        norm = jnp.sum(x * x, axis=1, keepdims=True) * (-LOG2E * 2.0 / FEAT)
        n0, n1, n2 = (v.astype(F32) for v in split3(norm))
        p0, p1, p2 = (v.astype(F32) for v in split3(x * (LOG2E * 8.0 / FEAT)))
        tail = jnp.where(lane == FEAT, n0, jnp.where(lane == FEAT + 1, n1, jnp.where(lane == FEAT + 2, n2, 0.0)))
        out_ref[pl.ds(at, rows), 0:HALF] = jnp.where(lane < FEAT, p0, p1).astype(BF16)
        out_ref[pl.ds(at, rows), HALF : 2 * HALF] = jnp.where(lane < FEAT, p2, tail).astype(BF16)
        return carry

    lax.fori_loop(0, count // rows, prepare, 0)


def arranged_rows(received, place_order):
    blocks, padded, _ = received.shape
    count = place_order.shape[0]
    half_rows = count // blocks // 2
    return pl.pallas_call(
        functools.partial(arranged_kernel, blocks=blocks, half_rows=half_rows),
        in_specs=[pl.BlockSpec(memory_space=pltpu.SMEM), pl.BlockSpec(memory_space=pltpu.VMEM)],
        out_shape=jax.ShapeDtypeStruct((count, 2 * HALF), BF16),
        scratch_shapes=[pltpu.VMEM((count, HALF), F32), pltpu.VMEM((count, HALF), F32)],
        compiler_params=pltpu.CompilerParams(vmem_limit_bytes=58 * MB),
        cost_estimate=pl.CostEstimate(flops=4 * 10**9, bytes_accessed=24 * MB, transcendentals=0),
        name="arranged_rows",
    )(place_order, received)


def sketch_kernel(left_ref, samples_ref, sk_ref, hi_ref, lo_ref, gram_ref, own_ref, wide, own):
    leaf = pl.program_id(0)
    owners, half_rows, _ = samples_ref.shape
    share = LEAF // owners
    slabs = half_rows // share

    @pl.when(leaf == 0)
    def _():
        wide[...] = samples_ref[...].astype(F32)
        own[...] = jnp.zeros_like(own)

    slab = wide[:, pl.ds(pl.multiple_of((leaf % slabs) * share, share), share), :].reshape(LEAF, HALF).astype(BF16)
    row = lax.broadcasted_iota(jnp.int32, (HALF, HALF), 0)
    col = lax.broadcasted_iota(jnp.int32, (HALF, HALF), 1)
    spread = jnp.where(row == (col % FEAT) + FEAT * (leaf // slabs), 1.0, 0.0).astype(BF16)
    s = jnp.dot(slab, spread, preferred_element_type=F32)
    s_hi, s_lo = split2(s * s)
    first = lax.broadcasted_iota(jnp.int32, (8, HALF), 1) < FEAT
    ones = jnp.where(first, 1.0, 0.0).astype(BF16)
    nt = (((1,), (1,)), ((), ()))
    norm = lax.dot_general(ones, s_hi, nt, preferred_element_type=F32)
    norm += lax.dot_general(ones, s_lo, nt, preferred_element_type=F32)
    norm = norm[0:1, :] * (-LOG2E * 4.0 / FEAT)
    lane = lax.broadcasted_iota(jnp.int32, (LEAF, HALF), 1)
    right = jnp.concatenate([s.astype(BF16), jnp.where(lane < FEAT, s, 1.0).astype(BF16)], axis=1)
    gram = jnp.zeros((RANK, 2 * RANK), F32)
    for c in range(LEAF // CHUNK):
        z = lax.dot_general(left_ref[c * CHUNK : (c + 1) * CHUNK, :], right, nt, preferred_element_type=F32)
        kern = jnp.exp2(z + norm).astype(BF16)
        sketched = jnp.dot(kern, sk_ref[...], preferred_element_type=F32)
        hi, lo = split2(sketched)
        hi_ref[c * CHUNK : (c + 1) * CHUNK, :] = hi
        lo_ref[c * CHUNK : (c + 1) * CHUNK, :] = lo
        gram += lax.dot_general(hi, jnp.concatenate([hi, lo], axis=1), (((0,), (0,)), ((), ())), preferred_element_type=F32)
    cross = gram[:, RANK:]
    gram = gram[:, :RANK] + cross + cross.T
    gram_ref[...] = gram
    own[...] += gram

    @pl.when(leaf == pl.num_programs(0) - 1)
    def _():
        cross_part, both, diagonal = pack_symmetric(own[...])
        own_ref[0:HALF, :] = cross_part
        own_ref[HALF : 2 * HALF, :] = both
        own_ref[2 * HALF : 2 * HALF + 8, :] = diagonal


def sketch_all(left, samples, sketch):
    rows = left.shape[0]
    n = rows // LEAF
    owners, half_rows, _ = samples.shape
    ordered = sketch.reshape(LEAF // owners, owners, RANK).transpose(1, 0, 2).reshape(LEAF, RANK)
    return pl.pallas_call(
        sketch_kernel,
        grid=(n,),
        in_specs=[
            pl.BlockSpec((LEAF, 2 * HALF), lambda i: (i, 0)),
            pl.BlockSpec((owners, half_rows, HALF), lambda i: (0, 0, 0)),
            pl.BlockSpec((LEAF, RANK), lambda i: (0, 0)),
        ],
        out_specs=[
            pl.BlockSpec((LEAF, RANK), lambda i: (i, 0)),
            pl.BlockSpec((LEAF, RANK), lambda i: (i, 0)),
            pl.BlockSpec((None, RANK, RANK), lambda i: (i, 0, 0)),
            pl.BlockSpec((2 * HALF + 8, HALF), lambda i: (0, 0)),
        ],
        out_shape=[
            jax.ShapeDtypeStruct((rows, RANK), BF16),
            jax.ShapeDtypeStruct((rows, RANK), BF16),
            jax.ShapeDtypeStruct((n, RANK, RANK), F32),
            jax.ShapeDtypeStruct((2 * HALF + 8, HALF), F32),
        ],
        scratch_shapes=[pltpu.VMEM((owners, half_rows, HALF), F32), pltpu.VMEM((RANK, RANK), F32)],
        compiler_params=pltpu.CompilerParams(vmem_limit_bytes=52 * MB),
        name="leaf_sketch",
    )(left, samples, ordered)


def load_grams(gram_ref, work):
    for m in range(BATCH):
        for h in range(2):
            work[h, m * RANK : (m + 1) * RANK, :] = gram_ref[m, :, h * HALF : (h + 1) * HALF]


def begin_kernel(gram_ref, work):
    load_grams(gram_ref, work)
    factor_all(work, last=FIRST_CUT)


def middle_kernel(state_ref, work):
    work[...] = state_ref[...]
    factor_all(work, first=FIRST_CUT, last=SECOND_CUT)


def factor_part(kernel, name, operand):
    return pl.pallas_call(
        kernel,
        out_shape=jax.ShapeDtypeStruct((2, BATCH * RANK, HALF), F32),
        compiler_params=pltpu.CompilerParams(vmem_limit_bytes=24 * MB),
        cost_estimate=pl.CostEstimate(flops=8 * 10**9, bytes_accessed=4 * MB, transcendentals=0),
        name=name,
    )(operand)


def basis_kernel(state_ref, hi_ref, lo_ref, out_ref, work, inv_hi, inv_lo):
    @pl.when(pl.program_id(0) == 0)
    def _():
        work[...] = state_ref[...]
        factor_all(work, first=SECOND_CUT)
        row = lax.broadcasted_iota(jnp.int32, (RANK, HALF), 0)
        col = lax.broadcasted_iota(jnp.int32, (RANK, HALF), 1)
        for m in range(BATCH):
            for h in range(2):
                value = work[h, m * RANK : (m + 1) * RANK, :] * math.sqrt(LEAF)
                value = jnp.where(row >= col + h * HALF, value, 0.0)
                hi, lo = split2(value)
                inv_hi[m, :, h * HALF : (h + 1) * HALF] = hi
                inv_lo[m, :, h * HALF : (h + 1) * HALF] = lo

    leaf = pl.program_id(0)
    dims = (((1,), (1,)), ((), ()))
    ih = inv_hi[leaf]
    il = inv_lo[leaf]
    for c in range(4):
        rows = slice(c * 256, (c + 1) * 256)
        hi = hi_ref[rows, :]
        value = lax.dot_general(hi, ih, dims, preferred_element_type=F32)
        value += lax.dot_general(hi, il, dims, preferred_element_type=F32)
        value += lax.dot_general(lo_ref[rows, :], ih, dims, preferred_element_type=F32)
        out_ref[rows, :] = value.astype(BF16)


def basis_all(state, hi, lo):
    rows = hi.shape[0]
    n = rows // LEAF
    assert n == BATCH
    return pl.pallas_call(
        basis_kernel,
        grid=(n,),
        in_specs=[
            pl.BlockSpec((2, BATCH * RANK, HALF), lambda i: (0, 0, 0)),
            pl.BlockSpec((LEAF, RANK), lambda i: (i, 0)),
            pl.BlockSpec((LEAF, RANK), lambda i: (i, 0)),
        ],
        out_specs=pl.BlockSpec((LEAF, RANK), lambda i: (i, 0)),
        out_shape=jax.ShapeDtypeStruct((rows, RANK), BF16),
        scratch_shapes=[
            pltpu.VMEM((2, BATCH * RANK, HALF), F32),
            pltpu.VMEM((BATCH, RANK, RANK), BF16),
            pltpu.VMEM((BATCH, RANK, RANK), BF16),
        ],
        compiler_params=pltpu.CompilerParams(vmem_limit_bytes=48 * MB),
        cost_estimate=pl.CostEstimate(flops=10 * 10**9, bytes_accessed=14 * MB, transcendentals=0),
        name="leaf_factor",
    )(state, hi, lo)


def pack_symmetric(gram):
    row = lax.broadcasted_iota(jnp.int32, (HALF, HALF), 0)
    col = lax.broadcasted_iota(jnp.int32, (HALF, HALF), 1)
    first = gram[:HALF, :HALF]
    last = gram[HALF:, HALF:]
    diagonal = jnp.sum(jnp.where(row == col, first, 0.0), axis=0, keepdims=True)
    return gram[:HALF, HALF:], jnp.where(row > col, first, last), jnp.broadcast_to(diagonal, (8, HALF))


def unpack_symmetric(packed):
    row = lax.broadcasted_iota(jnp.int32, (HALF, HALF), 0)
    col = lax.broadcasted_iota(jnp.int32, (HALF, HALF), 1)
    cross = packed[:HALF]
    both = packed[HALF : 2 * HALF]
    below = jnp.where(row > col, both, 0.0)
    above = jnp.where(row < col, both, 0.0)
    first = below + below.T + jnp.where(row == col, packed[2 * HALF : 2 * HALF + 1], 0.0)
    last = above + above.T + jnp.where(row == col, both, 0.0)
    return first, cross, last


def path_kernel(
    own_ref, pair_ref, near_ref, chips_ref, row_ref, plane_ref, one_ref, two_ref, three_ref, out_ref, work
):
    packed = [own_ref[...], pair_ref[...], pair_ref[...] + near_ref[...], chips_ref[...]]
    packed += [chips_ref[...] + row_ref[...], plane_ref[...]]
    packed.append(plane_ref[...] + one_ref[...])
    packed.append(packed[-1] + (two_ref[...] + three_ref[...]))
    for m in range(BATCH):
        first, cross, last = unpack_symmetric(packed[m])
        base = m * RANK
        work[0, base : base + HALF, :] = first
        work[1, base : base + HALF, :] = cross
        work[0, base + HALF : base + RANK, :] = cross.T
        work[1, base + HALF : base + RANK, :] = last
    factor_all(work)
    row = lax.broadcasted_iota(jnp.int32, (RANK, HALF), 0)
    col = lax.broadcasted_iota(jnp.int32, (RANK, HALF), 1)
    total = jnp.zeros((RANK, RANK), F32)
    dims = (((1,), (1,)), ((), ()))
    for m in range(BATCH - 1):
        up, inv = [], []
        for h in range(2):
            value = work[h, m * RANK : (m + 1) * RANK, :]
            diagonal = jnp.where(row == col + h * HALF, 1.0 / value, 0.0)
            up.append(jnp.where(row < col + h * HALF, value, diagonal))
            value = work[h, (m + 1) * RANK : (m + 2) * RANK, :]
            inv.append(jnp.where(row >= col + h * HALF, value, 0.0))
        uh, ul = split2(jnp.concatenate(up, axis=1))
        ih, il = split2(jnp.concatenate(inv, axis=1))
        total += lax.dot_general(uh, ih, dims, preferred_element_type=F32)
        total += lax.dot_general(uh, il, dims, preferred_element_type=F32)
        total += lax.dot_general(ul, ih, dims, preferred_element_type=F32)
    out_ref[...] = total

def path_all(*packed):
    return pl.pallas_call(
        path_kernel,
        out_shape=jax.ShapeDtypeStruct((RANK, RANK), F32),
        scratch_shapes=[
            pltpu.VMEM((2, BATCH * RANK, HALF), F32),
        ],
        compiler_params=pltpu.CompilerParams(vmem_limit_bytes=24 * MB),
        name="path_factor",
    )(*packed)


AXES = ("gx", "gy")


def partner(shard, axis, step):
    return lax.ppermute(shard, axis, [(i, i ^ step) for i in range(lax.axis_size(axis))])


def exchanged(blocks):
    return lax.all_to_all(blocks, AXES, split_axis=0, concat_axis=0, tiled=True)


def on_device(points, send_order, place_order, sample_rows, sketch):
    devices = lax.axis_size(AXES)
    received = exchanged(outgoing_rows(points, send_order, sample_rows, devices))
    samples = exchanged(picked_rows(received, place_order))
    left = arranged_rows(received, place_order)
    high, low, grams, own_gram = sketch_all(left, samples, sketch)
    pair = own_gram + partner(own_gram, "gy", 1)
    grams, pair = lax.optimization_barrier((grams, pair))
    near = [partner(pair, "gy", step) for step in (2, 4, 6)]
    state = factor_part(begin_kernel, "begin_factor", grams)
    chips = pair + near[0] + (near[1] + near[2])
    state, chips = lax.optimization_barrier((state, chips))
    rows = [partner(chips, "gx", step) for step in (1, 2, 3)]
    state = factor_part(middle_kernel, "middle_factor", state)
    plane = chips + rows[0] + (rows[1] + rows[2])
    state, plane = lax.optimization_barrier((state, plane))
    far = [partner(plane, "gx", step) for step in (4, 8, 12)]
    basis = basis_all(state, high, low)
    path = path_all(own_gram, pair, near[0], chips, rows[0], plane, *far)
    return (basis, path)


def solution(mesh):
    return jax.shard_map(
        on_device,
        mesh=mesh,
        in_specs=(P(AXES, None), P(AXES), P(AXES), P(AXES), P()),
        out_specs=(P(AXES, None), P(AXES, None)),
        check_vma=False,
    )
```

```python
import functools
import math

import jax
import jax.numpy as jnp
from jax import lax
from jax.experimental import pallas as pl
from jax.experimental.pallas import tpu as pltpu
from jax.sharding import PartitionSpec as P

LEAF = 1024
FEAT = 64
RANK = 256
HALF = 128
PANEL = 32
STEP = 8
BATCH = 8
FIRST_CUT = 3
SECOND_CUT = 6
CHUNK = 1024
LOG2E = 1.4426950408889634
MB = 1 << 20
F32 = jnp.float32
BF16 = jnp.bfloat16


def split2(x):
    hi = x.astype(BF16)
    return hi, (x - hi.astype(F32)).astype(BF16)


def split3(x):
    hi = x.astype(BF16)
    rest = x - hi.astype(F32)
    mid = rest.astype(BF16)
    return hi, mid, (rest - mid.astype(F32)).astype(BF16)


def eliminate(rows, half, offset):
    count = len(rows)
    shape = rows[0][0].shape
    lanes = lax.broadcasted_iota(jnp.int32, shape, 1) - offset

    def lane(row, at):
        return jnp.broadcast_to(row[half][:, offset + at : offset + at + 1], shape)

    def subtract(row, factor, pivot):
        return [row[h] - factor * pivot[h] for h in range(2)]

    for base in range(0, count, STEP):
        reach = min(2 * STEP, count - base)
        local = rows[base : base + STEP]
        coef = [
            [lane(local[i], base + j) if j >= i else None for j in range(reach)]
            for i in range(STEP)
        ]
        done = []
        lower = []
        for c in range(STEP):
            inv = lax.rsqrt(coef[c][c])
            for j in range(c + 1, reach):
                coef[c][j] = coef[c][j] * inv
            scaled = [local[c][h] * inv for h in range(2)]
            scaled[half] = jnp.where(lanes == base + c, inv, scaled[half])
            done.append(scaled)
            for i in range(c + 1, STEP):
                for j in range(i, reach):
                    coef[i][j] = coef[i][j] - coef[c][i] * coef[c][j]
                row = list(local[i])
                row[half] = jnp.where(lanes == base + c, 0.0, row[half])
                local[i] = subtract(row, coef[c][i], scaled)
            keep = list(scaled)
            keep[half] = jnp.where((lanes > base + c) & (lanes < base + STEP), 0.0, scaled[half])
            lower.append(keep)
        rows[base : base + STEP] = done
        for i in range(base + STEP, count):
            row = list(rows[i])
            row[half] = jnp.where((lanes >= base) & (lanes < base + STEP), 0.0, row[half])
            for c in range(STEP):
                factor = coef[c][i - base] if i - base < reach else lane(done[c], i)
                row = subtract(row, factor, lower[c])
            rows[i] = row
        yield


def factor_all(work, first=0, last=RANK // PANEL):
    waiting = []

    def unit_rows(begin):
        row = lax.broadcasted_iota(jnp.int32, (RANK - begin, RANK), 0)
        col = lax.broadcasted_iota(jnp.int32, (RANK - begin, RANK), 1)
        return jnp.where(row + begin == col, 1.0, 0.0).astype(BF16)

    def update(m, start, parts, low_row, high_row):
        half, offset = divmod(start, HALF)
        base = m * RANK
        left, rights = parts
        left = left[low_row - start - PANEL : high_row - start - PANEL]
        for g in range(2):
            prod = jnp.dot(left, rights[g], preferred_element_type=F32)
            old = work[g, base + low_row : base + high_row, :]
            if g == half:
                col = lax.broadcasted_iota(jnp.int32, old.shape, 1) - offset
                old = jnp.where((col >= 0) & (col < PANEL), 0.0, old)
            work[g, base + low_row : base + high_row, :] = old - prod

    for panel in range(first, last):
        start = panel * PANEL
        half, offset = divmod(start, HALF)
        rows = [[work[h, pl.ds(start + i, BATCH, stride=RANK), :] for h in range(2)] for i in range(PANEL)]
        groups = PANEL // STEP
        for step, _ in enumerate(eliminate(rows, half, offset)):
            share = -(-len(waiting) // (groups - step))
            for args in waiting[:share]:
                update(*args)
            waiting = waiting[share:]
        for i in range(PANEL):
            for h in range(2):
                work[h, pl.ds(start + i, BATCH, stride=RANK), :] = rows[i][h]
        after = start + PANEL
        if after == RANK:
            break
        col = lax.broadcasted_iota(jnp.int32, (PANEL, HALF), 1) - offset
        row = lax.broadcasted_iota(jnp.int32, (PANEL, HALF), 0)
        beyond = (col > row) & (col < PANEL)
        fresh = []
        for m in range(BATCH):
            parts = []
            for h in range(2):
                top = work[h, m * RANK + start : m * RANK + after, :]
                parts.append(split3(jnp.where(beyond, 0.0, top) if h == half else top))
            stack = [jnp.concatenate([hi, hi, mid, hi, mid, low], axis=0) for hi, mid, low in parts]
            mirror = lax.dot_general(
                unit_rows(after),
                jnp.concatenate(stack, axis=1),
                (((1,), (1,)), ((), ())),
                preferred_element_type=F32,
            )
            rights = [jnp.concatenate([hi, mid, hi, low, mid, hi], axis=0) for hi, mid, low in parts]
            fresh.append((mirror.astype(BF16), rights))
        for m in range(BATCH):
            update(m, start, fresh[m], after, after + PANEL)
        for m in range(BATCH):
            for h in range(2):
                low_row = max(after + PANEL, h * HALF)
                if low_row < (h + 1) * HALF:
                    waiting.append((m, start, fresh[m], low_row, (h + 1) * HALF))
        if panel == last - 1:
            for args in waiting:
                update(*args)


def duplicate(width, halves):
    row = lax.broadcasted_iota(jnp.int32, (width, HALF * halves), 0)
    col = lax.broadcasted_iota(jnp.int32, (width, HALF * halves), 1)
    return jnp.where(row == (col % FEAT) + FEAT * (col // HALF), 1.0, 0.0).astype(BF16)


def pack_rows(pick, table, packed, blocks, half_rows):
    low = lax.broadcasted_iota(jnp.int32, (1, HALF), 1) < FEAT

    def block(b, carry):
        for q in range(half_rows):
            one = table[pl.ds(pick(b, q), 1), :]
            two = table[pl.ds(pick(b, q + half_rows), 1), :]
            packed[pl.ds(b * half_rows + q, 1), :] = jnp.where(low, one, two)
        return carry

    lax.fori_loop(0, blocks, block, 0)


def emit_packed(packed, out_ref, blocks, half_rows):
    def block(b, carry):
        rows = packed[pl.ds(pl.multiple_of(b * half_rows, half_rows), half_rows), :]
        out_ref[b, 0:half_rows, :] = rows.astype(BF16)
        return carry

    lax.fori_loop(0, blocks, block, 0, unroll=8)


def outgoing_kernel(
    order_hbm, points_hbm, rows_hbm, out_ref, order_ref, points_ref, rows_ref, sem, table, packed, *, blocks, half_rows, extra
):
    features, count = points_ref.shape
    pairs = ((points_hbm, points_ref), (rows_hbm, rows_ref), (order_hbm, order_ref))
    copies = [pltpu.make_async_copy(src, dst, sem.at[k]) for k, (src, dst) in enumerate(pairs)]
    for copy in copies:
        copy.start()
    copies[0].wait()
    spread = duplicate(features, 1)
    piece = 1024

    def build(c, carry):
        at = pl.multiple_of(c * piece, piece)
        table[pl.ds(at, piece), :] = lax.dot_general(
            points_ref[:, pl.ds(at, piece)], spread, (((0,), (0,)), ((), ())), preferred_element_type=F32
        )
        return carry

    lax.fori_loop(0, count // piece, build, 0, unroll=2)
    copies[1].wait()
    wanted = rows_ref[...]
    high = (wanted >> 7).astype(F32)
    low = (wanted & 127).astype(F32)
    asked = jnp.concatenate([high, low], axis=0).T
    asked = jnp.concatenate([asked.reshape(blocks, 1, HALF), jnp.zeros((blocks, extra - 1, HALF), F32)], axis=1)
    out_ref[:, half_rows : half_rows + extra, :] = asked.astype(BF16)
    copies[2].wait()
    pack_rows(lambda b, q: order_ref[b * 2 * half_rows + q], table, packed, blocks, half_rows)
    emit_packed(packed, out_ref, blocks, half_rows)


def outgoing_rows(points, send_order, sample_rows, blocks):
    count, features = points.shape
    half_rows = count // blocks // 2
    extra = 8
    return pl.pallas_call(
        functools.partial(outgoing_kernel, blocks=blocks, half_rows=half_rows, extra=extra),
        in_specs=[pl.BlockSpec(memory_space=pl.ANY)] * 3,
        out_shape=jax.ShapeDtypeStruct((blocks, half_rows + extra, HALF), BF16),
        scratch_shapes=[
            pltpu.SMEM((count,), jnp.int32),
            pltpu.VMEM((features, count), BF16),
            pltpu.VMEM((count // blocks, blocks), jnp.int32),
            pltpu.SemaphoreType.DMA((3,)),
            pltpu.VMEM((count, HALF), F32),
            pltpu.VMEM((count // 2, HALF), F32),
        ],
        compiler_params=pltpu.CompilerParams(vmem_limit_bytes=58 * MB),
        name="outgoing_rows",
    )(send_order, points.T, sample_rows.reshape(-1, blocks))


def build_table(received_ref, table, blocks, half_rows):
    spread = duplicate(HALF, 2)

    def block(b, carry):
        both = jnp.dot(received_ref[b, 0:half_rows, :], spread, preferred_element_type=F32)
        at = pl.multiple_of(b * 2 * half_rows, 2 * half_rows)
        table[pl.ds(at, half_rows), :] = both[:, :HALF]
        table[pl.ds(at + half_rows, half_rows), :] = both[:, HALF:]
        return carry

    lax.fori_loop(0, blocks, block, 0, unroll=16)


def picked_kernel(place_ref, received_ref, out_ref, table, packed, asked, asked_smem, sem, *, blocks, half_rows):
    coded = received_ref[:, half_rows : half_rows + 1, :].astype(F32).reshape(blocks, HALF)
    asked[...] = (coded * 128.0 + pltpu.roll(coded, FEAT, 1)).astype(jnp.int32)
    copy = pltpu.make_async_copy(asked, asked_smem, sem)
    copy.start()
    build_table(received_ref, table, blocks, half_rows)
    copy.wait()
    pack_rows(lambda b, q: place_ref[asked_smem[b, q]], table, packed, blocks, half_rows)
    emit_packed(packed, out_ref, blocks, half_rows)


def picked_rows(received, place_order):
    blocks, padded, _ = received.shape
    count = place_order.shape[0]
    half_rows = count // blocks // 2
    return pl.pallas_call(
        functools.partial(picked_kernel, blocks=blocks, half_rows=half_rows),
        in_specs=[pl.BlockSpec(memory_space=pltpu.SMEM), pl.BlockSpec(memory_space=pltpu.VMEM)],
        out_shape=jax.ShapeDtypeStruct((blocks, half_rows, HALF), BF16),
        scratch_shapes=[
            pltpu.VMEM((count, HALF), F32),
            pltpu.VMEM((count // 2, HALF), F32),
            pltpu.VMEM((blocks, HALF), jnp.int32),
            pltpu.SMEM((blocks, HALF), jnp.int32),
            pltpu.SemaphoreType.DMA,
        ],
        compiler_params=pltpu.CompilerParams(vmem_limit_bytes=16 * MB),
        name="picked_rows",
    )(place_order, received)


def arranged_kernel(place_ref, received_ref, out_ref, table, moved, *, blocks, half_rows):
    build_table(received_ref, table, blocks, half_rows)
    count = out_ref.shape[0]
    piece = 64

    def move(b, carry):
        for q in range(piece):
            moved[pl.ds(b * piece + q, 1), :] = table[pl.ds(place_ref[b * piece + q], 1), :]
        return carry

    lax.fori_loop(0, count // piece, move, 0)
    rows = 128
    lane = lax.broadcasted_iota(jnp.int32, (rows, HALF), 1)

    def prepare(b, carry):
        at = pl.multiple_of(b * rows, rows)
        x = moved[pl.ds(at, rows), :]
        norm = jnp.sum(x * x, axis=1, keepdims=True) * (-LOG2E * 2.0 / FEAT)
        n0, n1, n2 = (v.astype(F32) for v in split3(norm))
        p0, p1, p2 = (v.astype(F32) for v in split3(x * (LOG2E * 8.0 / FEAT)))
        tail = jnp.where(lane == FEAT, n0, jnp.where(lane == FEAT + 1, n1, jnp.where(lane == FEAT + 2, n2, 0.0)))
        out_ref[pl.ds(at, rows), 0:HALF] = jnp.where(lane < FEAT, p0, p1).astype(BF16)
        out_ref[pl.ds(at, rows), HALF : 2 * HALF] = jnp.where(lane < FEAT, p2, tail).astype(BF16)
        return carry

    lax.fori_loop(0, count // rows, prepare, 0, unroll=4)


def arranged_rows(received, place_order):
    blocks, padded, _ = received.shape
    count = place_order.shape[0]
    half_rows = count // blocks // 2
    return pl.pallas_call(
        functools.partial(arranged_kernel, blocks=blocks, half_rows=half_rows),
        in_specs=[pl.BlockSpec(memory_space=pltpu.SMEM), pl.BlockSpec(memory_space=pltpu.VMEM)],
        out_shape=jax.ShapeDtypeStruct((count, 2 * HALF), BF16),
        scratch_shapes=[pltpu.VMEM((count, HALF), F32), pltpu.VMEM((count, HALF), F32)],
        compiler_params=pltpu.CompilerParams(vmem_limit_bytes=58 * MB),
        cost_estimate=pl.CostEstimate(flops=4 * 10**9, bytes_accessed=24 * MB, transcendentals=0),
        name="arranged_rows",
    )(place_order, received)


def sketch_kernel(left_ref, samples_ref, sk_ref, hi_ref, lo_ref, gram_ref, own_ref, wide, own):
    leaf = pl.program_id(0)
    owners, half_rows, _ = samples_ref.shape
    share = LEAF // owners
    slabs = half_rows // share

    @pl.when(leaf == 0)
    def _():
        wide[...] = samples_ref[...].astype(F32)
        own[...] = jnp.zeros_like(own)

    slab = wide[:, pl.ds(pl.multiple_of((leaf % slabs) * share, share), share), :].reshape(LEAF, HALF).astype(BF16)
    row = lax.broadcasted_iota(jnp.int32, (HALF, HALF), 0)
    col = lax.broadcasted_iota(jnp.int32, (HALF, HALF), 1)
    spread = jnp.where(row == (col % FEAT) + FEAT * (leaf // slabs), 1.0, 0.0).astype(BF16)
    s = jnp.dot(slab, spread, preferred_element_type=F32)
    s_hi, s_lo = split2(s * s)
    first = lax.broadcasted_iota(jnp.int32, (8, HALF), 1) < FEAT
    ones = jnp.where(first, 1.0, 0.0).astype(BF16)
    nt = (((1,), (1,)), ((), ()))
    norm = lax.dot_general(ones, s_hi, nt, preferred_element_type=F32)
    norm += lax.dot_general(ones, s_lo, nt, preferred_element_type=F32)
    norm = norm[0:1, :] * (-LOG2E * 4.0 / FEAT)
    lane = lax.broadcasted_iota(jnp.int32, (LEAF, HALF), 1)
    right = jnp.concatenate([s.astype(BF16), jnp.where(lane < FEAT, s, 1.0).astype(BF16)], axis=1)
    gram = jnp.zeros((RANK, 2 * RANK), F32)
    for c in range(LEAF // CHUNK):
        z = lax.dot_general(left_ref[c * CHUNK : (c + 1) * CHUNK, :], right, nt, preferred_element_type=F32)
        kern = jnp.exp2(z + norm).astype(BF16)
        sketched = jnp.dot(kern, sk_ref[...], preferred_element_type=F32)
        hi, lo = split2(sketched)
        hi_ref[c * CHUNK : (c + 1) * CHUNK, :] = hi
        lo_ref[c * CHUNK : (c + 1) * CHUNK, :] = lo
        gram += lax.dot_general(hi, jnp.concatenate([hi, lo], axis=1), (((0,), (0,)), ((), ())), preferred_element_type=F32)
    cross = gram[:, RANK:]
    gram = gram[:, :RANK] + cross + cross.T
    gram_ref[...] = gram
    own[...] += gram

    @pl.when(leaf == pl.num_programs(0) - 1)
    def _():
        cross_part, both, diagonal = pack_symmetric(own[...])
        own_ref[0:HALF, :] = cross_part
        own_ref[HALF : 2 * HALF, :] = both
        own_ref[2 * HALF : 2 * HALF + 8, :] = diagonal


def sketch_all(left, samples, sketch):
    rows = left.shape[0]
    n = rows // LEAF
    owners, half_rows, _ = samples.shape
    ordered = sketch.reshape(LEAF // owners, owners, RANK).transpose(1, 0, 2).reshape(LEAF, RANK)
    return pl.pallas_call(
        sketch_kernel,
        grid=(n,),
        in_specs=[
            pl.BlockSpec((LEAF, 2 * HALF), lambda i: (i, 0)),
            pl.BlockSpec((owners, half_rows, HALF), lambda i: (0, 0, 0)),
            pl.BlockSpec((LEAF, RANK), lambda i: (0, 0)),
        ],
        out_specs=[
            pl.BlockSpec((LEAF, RANK), lambda i: (i, 0)),
            pl.BlockSpec((LEAF, RANK), lambda i: (i, 0)),
            pl.BlockSpec((None, RANK, RANK), lambda i: (i, 0, 0)),
            pl.BlockSpec((2 * HALF + 8, HALF), lambda i: (0, 0)),
        ],
        out_shape=[
            jax.ShapeDtypeStruct((rows, RANK), BF16),
            jax.ShapeDtypeStruct((rows, RANK), BF16),
            jax.ShapeDtypeStruct((n, RANK, RANK), F32),
            jax.ShapeDtypeStruct((2 * HALF + 8, HALF), F32),
        ],
        scratch_shapes=[pltpu.VMEM((owners, half_rows, HALF), F32), pltpu.VMEM((RANK, RANK), F32)],
        compiler_params=pltpu.CompilerParams(vmem_limit_bytes=48 * MB),
        name="leaf_sketch",
    )(left, samples, ordered)


def load_grams(gram_ref, work):
    for m in range(BATCH):
        for h in range(2):
            work[h, m * RANK : (m + 1) * RANK, :] = gram_ref[m, :, h * HALF : (h + 1) * HALF]


def begin_kernel(gram_ref, work):
    load_grams(gram_ref, work)
    factor_all(work, last=FIRST_CUT)


def middle_kernel(state_ref, work):
    work[...] = state_ref[...]
    factor_all(work, first=FIRST_CUT, last=SECOND_CUT)


def factor_part(kernel, name, operand):
    return pl.pallas_call(
        kernel,
        out_shape=jax.ShapeDtypeStruct((2, BATCH * RANK, HALF), F32),
        compiler_params=pltpu.CompilerParams(vmem_limit_bytes=24 * MB),
        cost_estimate=pl.CostEstimate(flops=8 * 10**9, bytes_accessed=4 * MB, transcendentals=0),
        name=name,
    )(operand)


def basis_kernel(state_ref, high_ref, low_ref, basis_ref, high, low, basis, in_sem, out_sem, work):
    def span(leaf):
        return pl.ds(leaf * LEAF, LEAF)

    loads = [
        [
            pltpu.make_async_copy(src.at[span(leaf), :], dst.at[span(leaf), :], in_sem.at[leaf, k])
            for k, (src, dst) in enumerate(((high_ref, high), (low_ref, low)))
        ]
        for leaf in range(BATCH)
    ]
    stores = [
        pltpu.make_async_copy(basis.at[span(leaf), :], basis_ref.at[span(leaf), :], out_sem.at[leaf])
        for leaf in range(BATCH)
    ]
    for pair in loads:
        for copy in pair:
            copy.start()
    work[...] = state_ref[...]
    factor_all(work, first=SECOND_CUT)
    row = lax.broadcasted_iota(jnp.int32, (RANK, HALF), 0)
    col = lax.broadcasted_iota(jnp.int32, (RANK, HALF), 1)
    dims = (((1,), (1,)), ((), ()))
    for leaf in range(BATCH):
        inverse = []
        for h in range(2):
            value = work[h, leaf * RANK : (leaf + 1) * RANK, :] * math.sqrt(LEAF)
            inverse.append(jnp.where(row >= col + h * HALF, value, 0.0))
        ih, il = split2(jnp.concatenate(inverse, axis=1))
        for copy in loads[leaf]:
            copy.wait()
        for c in range(LEAF // RANK):
            rows = slice(leaf * LEAF + c * RANK, leaf * LEAF + (c + 1) * RANK)
            part = high[rows, :]
            value = lax.dot_general(part, ih, dims, preferred_element_type=F32)
            value += lax.dot_general(part, il, dims, preferred_element_type=F32)
            value += lax.dot_general(low[rows, :], ih, dims, preferred_element_type=F32)
            basis[rows, :] = value.astype(BF16)
        stores[leaf].start()
    for copy in stores:
        copy.wait()


def basis_all(state, high, low):
    rows = high.shape[0]
    assert rows == BATCH * LEAF
    anywhere = pl.BlockSpec(memory_space=pl.ANY)
    return pl.pallas_call(
        basis_kernel,
        in_specs=[pl.BlockSpec(memory_space=pltpu.VMEM), anywhere, anywhere],
        out_specs=anywhere,
        out_shape=jax.ShapeDtypeStruct((rows, RANK), BF16),
        scratch_shapes=[
            pltpu.VMEM((rows, RANK), BF16),
            pltpu.VMEM((rows, RANK), BF16),
            pltpu.VMEM((rows, RANK), BF16),
            pltpu.SemaphoreType.DMA((BATCH, 2)),
            pltpu.SemaphoreType.DMA((BATCH,)),
            pltpu.VMEM((2, BATCH * RANK, HALF), F32),
        ],
        compiler_params=pltpu.CompilerParams(vmem_limit_bytes=48 * MB),
        cost_estimate=pl.CostEstimate(flops=10 * 10**9, bytes_accessed=14 * MB, transcendentals=0),
        name="leaf_factor",
    )(state, high, low)


def pack_symmetric(gram):
    row = lax.broadcasted_iota(jnp.int32, (HALF, HALF), 0)
    col = lax.broadcasted_iota(jnp.int32, (HALF, HALF), 1)
    first = gram[:HALF, :HALF]
    last = gram[HALF:, HALF:]
    diagonal = jnp.sum(jnp.where(row == col, first, 0.0), axis=0, keepdims=True)
    return gram[:HALF, HALF:], jnp.where(row > col, first, last), jnp.broadcast_to(diagonal, (8, HALF))


def unpack_symmetric(packed):
    row = lax.broadcasted_iota(jnp.int32, (HALF, HALF), 0)
    col = lax.broadcasted_iota(jnp.int32, (HALF, HALF), 1)
    cross = packed[:HALF]
    both = packed[HALF : 2 * HALF]
    below = jnp.where(row > col, both, 0.0)
    above = jnp.where(row < col, both, 0.0)
    first = below + below.T + jnp.where(row == col, packed[2 * HALF : 2 * HALF + 1], 0.0)
    last = above + above.T + jnp.where(row == col, both, 0.0)
    return first, cross, last


def path_kernel(
    own_ref, pair_ref, near_ref, chips_ref, row_ref, plane_ref, one_ref, two_ref, three_ref, out_ref, work
):
    packed = [own_ref[...], pair_ref[...], pair_ref[...] + near_ref[...], chips_ref[...]]
    packed += [chips_ref[...] + row_ref[...], plane_ref[...]]
    packed.append(plane_ref[...] + one_ref[...])
    packed.append(packed[-1] + (two_ref[...] + three_ref[...]))
    for m in range(BATCH):
        first, cross, last = unpack_symmetric(packed[m])
        base = m * RANK
        work[0, base : base + HALF, :] = first
        work[1, base : base + HALF, :] = cross
        work[0, base + HALF : base + RANK, :] = cross.T
        work[1, base + HALF : base + RANK, :] = last
    factor_all(work)
    row = lax.broadcasted_iota(jnp.int32, (RANK, HALF), 0)
    col = lax.broadcasted_iota(jnp.int32, (RANK, HALF), 1)
    total = jnp.zeros((RANK, RANK), F32)
    dims = (((1,), (1,)), ((), ()))
    for m in range(BATCH - 1):
        up, inv = [], []
        for h in range(2):
            value = work[h, m * RANK : (m + 1) * RANK, :]
            diagonal = jnp.where(row == col + h * HALF, 1.0 / value, 0.0)
            up.append(jnp.where(row < col + h * HALF, value, diagonal))
            value = work[h, (m + 1) * RANK : (m + 2) * RANK, :]
            inv.append(jnp.where(row >= col + h * HALF, value, 0.0))
        uh, ul = split2(jnp.concatenate(up, axis=1))
        ih, il = split2(jnp.concatenate(inv, axis=1))
        total += lax.dot_general(uh, ih, dims, preferred_element_type=F32)
        total += lax.dot_general(uh, il, dims, preferred_element_type=F32)
        total += lax.dot_general(ul, ih, dims, preferred_element_type=F32)
    out_ref[...] = total

def path_all(*packed):
    return pl.pallas_call(
        path_kernel,
        out_shape=jax.ShapeDtypeStruct((RANK, RANK), F32),
        scratch_shapes=[
            pltpu.VMEM((2, BATCH * RANK, HALF), F32),
        ],
        compiler_params=pltpu.CompilerParams(vmem_limit_bytes=24 * MB),
        name="path_factor",
    )(*packed)


AXES = ("gx", "gy")


def partner(shard, axis, step):
    return lax.ppermute(shard, axis, [(i, i ^ step) for i in range(lax.axis_size(axis))])


def exchanged(blocks):
    return lax.all_to_all(blocks, AXES, split_axis=0, concat_axis=0, tiled=True)


def on_device(points, send_order, place_order, sample_rows, sketch):
    devices = lax.axis_size(AXES)
    received = exchanged(outgoing_rows(points, send_order, sample_rows, devices))
    samples = exchanged(picked_rows(received, place_order))
    left = arranged_rows(received, place_order)
    high, low, grams, own_gram = sketch_all(left, samples, sketch)
    pair = own_gram + partner(own_gram, "gy", 1)
    grams, pair = lax.optimization_barrier((grams, pair))
    near = [partner(pair, "gy", step) for step in (2, 4, 6)]
    state = factor_part(begin_kernel, "begin_factor", grams)
    chips = pair + near[0] + (near[1] + near[2])
    state, chips = lax.optimization_barrier((state, chips))
    rows = [partner(chips, "gx", step) for step in (1, 2, 3)]
    state = factor_part(middle_kernel, "middle_factor", state)
    plane = chips + rows[0] + (rows[1] + rows[2])
    state, plane = lax.optimization_barrier((state, plane))
    far = [partner(plane, "gx", step) for step in (4, 8, 12)]
    basis = basis_all(state, high, low)
    path = path_all(own_gram, pair, near[0], chips, rows[0], plane, *far)
    return (basis, path)


def solution(mesh):
    return jax.shard_map(
        on_device,
        mesh=mesh,
        in_specs=(P(AXES, None), P(AXES), P(AXES), P(AXES), P()),
        out_specs=(P(AXES, None), P(AXES, None)),
        check_vma=False,
    )
```
